128 devices in a mesh: section: 4 (over y_hi, core), dp: 32 (over y_lo, x, z).
Axes of the slice: x: 4, y: 4 (y_hi: 2, y_lo: 2; y = y_hi * 2 + y_lo), z: 4, core: 2. Of those that a mesh axis runs over, the one named last changes fastest.
Arguments:
- entry_states: bfloat16 [5, 1024, 4608], P(None, 'dp'), may hold values from -6 to 6
- down_proj: bfloat16 [4, 4, 4608, 128], P('section'), may hold values from -0.09375 to 0.09375
- up_proj: bfloat16 [4, 4, 4608, 128], P('section'), may hold values from -0.5 to 0.5
- label_rows: bfloat16 [256, 4608], replicated, may hold values from -0.375 to 0.375
- sampled_labels: int32 [4, 5, 1024], P(None, None, 'dp'), may hold values from 0 to 255
- eval_states: bfloat16 [1024, 4608], P('dp'), may hold values from -6 to 6
Outputs:
- eval_out: bfloat16 [4, 1024, 4608], P('section', 'dp')
- label_logprob: float32 [4, 5, 1024], P('section', None, 'dp')
- fisher_log: float32 [4, 2, 4608, 128], P('section', None, 'dp')
The draws below stay inside these ranges and needn't reach their ends.
All inputs are finite; a program needn't handle non-finite values.
Results may differ from the reference program's by a relative error of at most 0.0065.
Values may be sent and summed in bfloat16 or wider, within the bound.
A program may use at most 128 MiB of HBM per device.

```python
import jax
import jax.numpy as jnp
from jax import lax

D = 4608
R = 128
LABELS = 256
TASKS = 4
MICRO = 5
SECTIONS = 4
TOKENS = 1024
EVAL = 1024


def touch_ends(values, rng, low, largest):
    dims = values.shape
    index_at = [jax.random.randint(jax.random.fold_in(rng, axis), (), 0, dims[axis]) for axis in range(len(dims))]
    values = values.at[tuple(index_at)].set(low)
    longest = dims.index(max(dims))
    index_at[longest] = (index_at[longest] + 1) % dims[longest]
    return values.at[tuple(index_at)].set(largest)


def strengthened(entries, stream_key, source, target, parts, factor):
    def block_of(position):
        return (jnp.arange(entries.shape[position]) // (entries.shape[position] // parts)).reshape((-1,) + (1,) * (entries.ndim - 1 - position))

    first = jax.random.permutation(stream_key, parts)[block_of(target)]
    other_side = (block_of(target) + parts // 2) % parts
    return jnp.where((block_of(source) == first) | (block_of(source) == other_side), factor * entries, entries)


def block_levels(rng, dims, pieces, low, top_value):
    level, own = 1.0, jax.random.fold_in(rng, 6)
    for dim, blocks in pieces:
        steps = jnp.exp(jax.random.uniform(jax.random.fold_in(own, dim), (blocks,), jnp.float32, low / len(pieces), top_value / len(pieces)))
        level = level * jnp.repeat(steps, dims[dim] // blocks).reshape([-1 if axis == dim else 1 for axis in range(len(dims))])
    return level


def centred(rng, dims, width, most, split=(), kind=jnp.bfloat16):
    drawn = width * jax.random.normal(rng, dims, jnp.float32)
    if split:
        drawn = drawn * block_levels(rng, dims, split, -0.22, 0.18)
    return jnp.clip(drawn, -most, most).astype(kind)


def noise_with(own_key, shape, width, limit, cuts, heavy, held_as=jnp.bfloat16):
    values = width * jax.random.normal(own_key, shape, jnp.float32)
    if cuts:
        values = values * block_levels(own_key, shape, cuts, -0.22, 0.18)
    return jnp.clip(strengthened(values, jax.random.fold_in(own_key, 3), *heavy), -limit, limit).astype(held_as)


def setup_inputs(seed: int = 0) -> dict:
    streams_of = jax.random.split(jax.random.key(seed), 7)
    return {
        "entry_states": noise_with(streams_of[0], (MICRO, TOKENS, D), 1.0, 6.0, ((1, 32),), (1, 2, 32, 2.75)),
        "down_proj": centred(streams_of[1], (SECTIONS, TASKS, D, R), D ** -0.5, 0.09375, ((0, 4),)),
        "up_proj": centred(streams_of[2], (SECTIONS, TASKS, D, R), R ** -0.5, 0.5, ((0, 4),)),
        "label_rows": centred(streams_of[3], (LABELS, D), (D // 16) ** -0.5, 0.375),
        "sampled_labels": touch_ends(jax.random.randint(streams_of[4], (TASKS, MICRO, TOKENS), 0, LABELS), jax.random.fold_in(streams_of[4], 1), 0, LABELS - 1).astype(jnp.int32),
        "eval_states": centred(streams_of[5], (EVAL, D), 1.0, 6.0, ((0, 32),)),
    }


norm_eps = 1e-06
merge_eps = 1e-06
soft_cap = 30.0
gelu_coef = 0.7978845608028654

def gelu_value(hidden):
    gelu_inner = gelu_coef * (hidden + 0.044715 * hidden * hidden * hidden)
    return 0.5 * hidden * (1.0 + jnp.tanh(gelu_inner))

def gelu_slope(hidden):
    gelu_inner = gelu_coef * (hidden + 0.044715 * hidden * hidden * hidden)
    tanh_value = jnp.tanh(gelu_inner)
    return 0.5 * (1.0 + tanh_value) + 0.5 * hidden * (1.0 - tanh_value * tanh_value) * gelu_coef * (1.0 + 3.0 * 0.044715 * hidden * hidden)

def block_forward(states, w_down, w_up):
    state_float = states.astype(jnp.float32)
    norm_scale = lax.rsqrt(lax.optimization_barrier(jnp.mean(state_float * state_float, axis=-1, keepdims=True)) + norm_eps)
    norm_float = state_float * norm_scale
    normed = norm_float.astype(jnp.bfloat16)
    hidden = jnp.einsum('tnd,tdr->tnr', normed.astype(jnp.float32), w_down.astype(jnp.float32))
    active = gelu_value(hidden).astype(jnp.bfloat16)
    update = jnp.einsum('tnr,tdr->tnd', active.astype(jnp.float32), w_up.astype(jnp.float32))
    output = (state_float + update).astype(jnp.bfloat16)
    return (output, (normed, norm_float, norm_scale, hidden, active))

def label_head(states, labels, label_rows):
    state_float = states.astype(jnp.float32)
    norm_scale = lax.rsqrt(lax.optimization_barrier(jnp.mean(state_float * state_float, axis=-1, keepdims=True)) + norm_eps)
    norm_float = state_float * norm_scale
    normed = norm_float.astype(jnp.bfloat16)
    logits = jnp.einsum('tnd,ld->tnl', normed.astype(jnp.float32), label_rows.astype(jnp.float32))
    tanh_bent = jnp.tanh(logits / soft_cap)
    capped = soft_cap * tanh_bent
    logprob_all = capped - jnp.log(lax.optimization_barrier(jnp.sum(jnp.exp(capped), axis=-1, keepdims=True)))
    one_hot = (labels[..., None] == jnp.arange(logprob_all.shape[-1], dtype=jnp.int32)).astype(jnp.float32)
    picked = lax.optimization_barrier(jnp.sum(logprob_all * one_hot, axis=-1))
    logit_slope = ((jnp.exp(logprob_all) - one_hot) * (1.0 - tanh_bent * tanh_bent)).astype(jnp.bfloat16)
    grad_norm = jnp.einsum('tnl,ld->tnd', logit_slope.astype(jnp.float32), label_rows.astype(jnp.float32))
    grad_states = (norm_scale * (grad_norm - norm_float * lax.optimization_barrier(jnp.mean(grad_norm * norm_float, axis=-1, keepdims=True)))).astype(jnp.bfloat16)
    return (grad_states, picked)

def block_backward(grad_out, saved, w_down, w_up):
    normed, norm_float, norm_scale, hidden, active = saved
    grad_float = grad_out.astype(jnp.float32)
    grad_act = jnp.einsum('tnd,tdr->tnr', grad_float, w_up.astype(jnp.float32))
    grad_hidden = (grad_act * gelu_slope(hidden)).astype(jnp.bfloat16)
    grad_norm = jnp.einsum('tnr,tdr->tnd', grad_hidden.astype(jnp.float32), w_down.astype(jnp.float32))
    grad_in = (grad_float + norm_scale * (grad_norm - norm_float * lax.optimization_barrier(jnp.mean(grad_norm * norm_float, axis=-1, keepdims=True)))).astype(jnp.bfloat16)
    normed_float = normed.astype(jnp.float32)
    hidden_float = grad_hidden.astype(jnp.float32)
    active_float = active.astype(jnp.float32)
    wide_square = jnp.stack([normed_float * normed_float, grad_float * grad_float], axis=1).astype(jnp.bfloat16)
    narrow_square = jnp.stack([hidden_float * hidden_float, active_float * active_float], axis=1).astype(jnp.bfloat16)
    return (grad_in, wide_square, narrow_square)

def reference(entry_states, down_proj, up_proj, label_rows, sampled_labels, eval_states):
    section_count = down_proj.shape[0]
    fisher = jnp.zeros((section_count, TASKS, 2, D, R), jnp.float32)
    picked_all = []
    for micro_index in range(MICRO):
        states = jnp.broadcast_to(entry_states[micro_index][None], (TASKS, TOKENS, D))
        inputs = []
        for section_step in range(section_count):
            inputs.append(states)
            states, _ = block_forward(states, down_proj[section_step], up_proj[section_step])
        grad_out, picked = label_head(states, sampled_labels[:, micro_index, :], label_rows)
        picked_all.append(picked)
        for section_step in reversed(range(section_count)):
            _, saved = block_forward(inputs[section_step], down_proj[section_step], up_proj[section_step])
            grad_out, wide_square, narrow_square = block_backward(grad_out, saved, down_proj[section_step], up_proj[section_step])
            term = jnp.einsum('tknd,tknr->tkdr', wide_square.astype(jnp.float32), narrow_square.astype(jnp.float32))
            fisher = fisher.at[section_step].add(term)
    label_logprob = jnp.stack(picked_all, axis=1)
    stacked = jnp.stack([down_proj, up_proj], axis=2).astype(jnp.float32)
    numerator = lax.optimization_barrier(jnp.sum(fisher * stacked, axis=1))
    denominator = lax.optimization_barrier(jnp.sum(fisher, axis=1))
    merged = (numerator / (denominator + merge_eps)).astype(jnp.bfloat16)
    fisher_log = jnp.log(denominator + merge_eps)
    current = eval_states[None]
    outputs = []
    for section_step in range(section_count):
        current, _ = block_forward(current, merged[section_step, 0][None], merged[section_step, 1][None])
        outputs.append(current[0])
    eval_out = jnp.stack(outputs, axis=0)
    return (eval_out, label_logprob, fisher_log)
```

```python
import jax
import jax.numpy as jnp
from jax import lax
from jax.experimental import pallas as pl
from jax.experimental.pallas import tpu as pltpu
from jax.sharding import PartitionSpec as P

norm_eps = 1e-06
merge_eps = 1e-06
soft_cap = 30.0
gelu_coef = 0.7978845608028654

D = 4608
R = 128
LABELS = 256
TASKS = 4
MICRO = 5
ROWS = 32
N = MICRO * ROWS
TILE = 512
BLK = D // 4
F32 = jnp.float32
BF16 = jnp.bfloat16
MESH = pl.DeviceIdType.MESH


def gelu_value(hidden):
    inner = gelu_coef * (hidden + 0.044715 * hidden * hidden * hidden)
    return 0.5 * hidden * (1.0 + jnp.tanh(inner))


def gelu_slope(hidden):
    inner = gelu_coef * (hidden + 0.044715 * hidden * hidden * hidden)
    t = jnp.tanh(inner)
    return 0.5 * (1.0 + t) + 0.5 * hidden * (1.0 - t * t) * gelu_coef * (
        1.0 + 3.0 * 0.044715 * hidden * hidden
    )


def dot_nn(a, b):
    return lax.dot_general(a, b, (((1,), (0,)), ((), ())), preferred_element_type=F32)


def dot_nt(a, b):
    return lax.dot_general(a, b, (((1,), (1,)), ((), ())), preferred_element_type=F32)


def dot_tn(a, b):
    return lax.dot_general(a, b, (((0,), (0,)), ((), ())), preferred_element_type=F32)


def lane_fold(v):
    total = v[:, 0:128]
    for i in range(1, v.shape[1] // 128):
        total = total + v[:, i * 128 : (i + 1) * 128]
    return total


def kernel(
    down, up, entry, labels, label_rows, evals,
    eval_out, logp_out, flog_out,
    w, x, g, rows, lab, n2, g2, hid, act, scale,
    fb, r1, r2, s2, r3, s3, r4, wd, merged, vin, picked,
    load_sem, ps, pr, cs, cr, as_, ar, bs, br, os_, orr, es, er, fs, fr,
    s1s, s1r, s2s, s2r, ys, yr, gs, gr, vs, vr,
):
    s = lax.axis_index("section")
    d = lax.axis_index("dp")
    h = s // 2
    c = s % 2
    yl = d // 16
    xx = (d // 4) % 4
    zz = d % 4
    y = 2 * h + yl
    u = xx * (1 - c) + zz * c
    v = zz * (1 - c) + xx * c

    def at(h_, c_, yl_, x_, z_):
        return {"section": h_ * 2 + c_, "dp": yl_ * 16 + x_ * 4 + z_}

    def at_uv(u_, v_):
        return at(h, c, yl, u_ * (1 - c) + v_ * c, v_ * (1 - c) + u_ * c)

    def at_y(y_):
        return at(y_ // 2, c, y_ % 2, xx, zz)

    partner = at(h, 1 - c, yl, xx, zz)
    swap = at(h, 1 - c, 1 - yl, xx, zz)
    across = at(1 - h, c, 1 - yl, xx, zz)
    after = at(1 - h, 1 - c, yl, xx, zz)
    a_peers = [None] + [at_uv((u + i) % 4, v) for i in range(1, 4)]
    b_peers = [None] + [at_uv(u, (v + i) % 4) for i in range(1, 4)]
    y_peers = [None] + [at_y((y + i) % 4) for i in range(1, 4)]

    def remote(src, dst, send, recv, to):
        return pltpu.make_async_remote_copy(
            src_ref=src, dst_ref=dst, send_sem=send, recv_sem=recv, device_id=to, device_id_type=MESH
        )

    barrier = pltpu.get_barrier_semaphore()
    everyone = [partner, swap, after] + a_peers[1:] + b_peers[1:] + y_peers[1:]
    for peer in everyone:
        pl.semaphore_signal(barrier, inc=1, device_id=peer, device_id_type=MESH)
    pl.semaphore_wait(barrier, len(everyone))

    far = 3 - y
    own = u * 4 + v
    part = D // 16
    slice_rows = pl.ds(own * part, part)
    cross = [
        remote(down.at[far, slice_rows], w.at[s, 0, slice_rows], cs.at[0], cr.at[0], across),
        remote(up.at[far, slice_rows], w.at[s, 1, slice_rows], cs.at[1], cr.at[1], across),
    ]
    for copy in cross:
        copy.start()
    beside = [
        remote(down.at[y], w.at[s, 0], ps.at[0], pr.at[0], partner),
        remote(up.at[y], w.at[s, 1], ps.at[1], pr.at[1], partner),
    ]
    moved = [
        remote(entry, x.at[0], es.at[0], er.at[0], swap),
        remote(labels.at[2 * h + 1 - yl], lab, es.at[1], er.at[1], swap),
    ]
    kept = [
        pltpu.make_async_copy(entry, x.at[0], load_sem.at[0]),
        pltpu.make_async_copy(labels.at[y], lab, load_sem.at[1]),
    ]

    @pl.when(c != yl)
    def _():
        for copy in moved:
            copy.start()

    @pl.when(c == yl)
    def _():
        for copy in kept:
            copy.start()

    for copy in beside:
        copy.start()
    loads = [
        pltpu.make_async_copy(down.at[y], w.at[s, 0], load_sem.at[2]),
        pltpu.make_async_copy(up.at[y], w.at[s, 1], load_sem.at[3]),
        pltpu.make_async_copy(label_rows, rows, load_sem.at[4]),
    ]
    mine = pl.ds(pl.multiple_of(d * 144, 16), 144)
    for t in range(TASKS):
        loads.append(pltpu.make_async_copy(down.at[t, mine], wd.at[t, 0], load_sem.at[5 + 2 * t]))
        loads.append(pltpu.make_async_copy(up.at[t, mine], wd.at[t, 1], load_sem.at[6 + 2 * t]))
    for copy in loads:
        copy.start()
    eval_load = pltpu.make_async_copy(evals, vin, load_sem.at[13])

    @pl.when(s == 0)
    def _():
        eval_load.start()

    lr = 2 * (1 - h) + c

    def piece(u_, v_):
        return w.at[lr, :, pl.ds((u_ * 4 + v_) * part, part)]

    for copy in cross:
        copy.wait_recv()
    a_sends = []
    for i in range(1, 4):
        copy = remote(piece(u, v), piece(u, v), as_.at[i], ar.at[i], a_peers[i])
        copy.start()
        a_sends.append(copy)
    b_sends = []
    for i in range(4):
        if i:
            from_u = (u + 4 - i) % 4
            remote(piece(from_u, v), piece(from_u, v), as_.at[i], ar.at[i], a_peers[i]).wait_recv()
        else:
            from_u = u
        for j in range(1, 4):
            copy = remote(piece(from_u, v), piece(from_u, v), bs.at[i, j], br.at[i, j], b_peers[j])
            copy.start()
            b_sends.append(copy)
    o_sends = []
    for i in range(4):
        from_u = (u + 4 - i) % 4
        for j in range(1, 4):
            from_v = (v + 4 - j) % 4
            remote(piece(from_u, from_v), piece(from_u, from_v), bs.at[i, j], br.at[i, j], b_peers[j]).wait_recv()
        block = w.at[lr, :, pl.ds(from_u * BLK, BLK)]
        copy = remote(block, block, os_.at[i], orr.at[i], partner)
        copy.start()
        o_sends.append(copy)

    @pl.when(c != yl)
    def _():
        for copy in moved:
            copy.wait()

    @pl.when(c == yl)
    def _():
        for copy in kept:
            copy.wait()

    for copy in beside:
        copy.wait()
    for copy in loads:
        copy.wait()
    for copy in cross + a_sends + b_sends:
        copy.wait_send()
    for copy in o_sends:
        copy.wait()

    zero = jnp.zeros((N, 128), F32)

    def cols(f, size=TILE):
        return pl.ds(pl.multiple_of(f * size, size), size)

    def first(f, carry):
        total, acc = carry
        xt = x[0, :, cols(f)]
        xf = xt.astype(F32)
        return total + lane_fold(xf * xf), acc + dot_nn(xt, w[0, 0, cols(f), :])

    total, acc = lax.fori_loop(0, D // TILE, first, (zero, zero))
    for k in range(4):
        sk = lax.rsqrt(jnp.sum(total, axis=1, keepdims=True) * (1.0 / D) + norm_eps)
        hk = sk * acc
        scale[k] = jnp.broadcast_to(sk, (N, 128))
        hid[k] = hk
        ak = gelu_value(hk).astype(BF16)
        act[k] = ak

        def step(f, carry, k=k, ak=ak):
            total, acc = carry
            new = (x[k, :, cols(f)].astype(F32) + dot_nt(ak, w[k, 1, cols(f), :])).astype(BF16)
            x[k + 1, :, cols(f)] = new
            nf = new.astype(F32)
            if k < 3:
                more = dot_nn(new, w[k + 1, 0, cols(f), :])
            else:
                more = dot_nt(new, rows[:, cols(f)])
            return total + lane_fold(nf * nf), acc + more

        width = R if k < 3 else LABELS
        total, acc = lax.fori_loop(0, D // TILE, step, (zero, jnp.zeros((N, width), F32)))

    sy = lax.rsqrt(jnp.sum(total, axis=1, keepdims=True) * (1.0 / D) + norm_eps)
    logits = sy * acc
    bent = jnp.tanh(logits * (1.0 / soft_cap))
    capped = soft_cap * bent
    logp = capped - jnp.log(jnp.sum(jnp.exp(capped), axis=1, keepdims=True))
    hot = lab[:, 0:1] == lax.broadcasted_iota(jnp.int32, (N, LABELS), 1)
    chosen = jnp.sum(jnp.where(hot, logp, 0.0), axis=1, keepdims=True)
    picked[...] = jnp.broadcast_to(chosen, (N, 128))
    give = remote(picked, logp_out, es.at[2], er.at[2], swap)
    hold = pltpu.make_async_copy(picked, logp_out, load_sem.at[14])

    @pl.when(c != yl)
    def _():
        give.start()

    @pl.when(c == yl)
    def _():
        hold.start()

    e = ((jnp.exp(logp) - jnp.where(hot, 1.0, 0.0)) * (1.0 - bent * bent)).astype(BF16)
    mean = jnp.sum(e.astype(F32) * logits, axis=1, keepdims=True) * (1.0 / D)
    sm = sy * mean

    def head(f, acc):
        back = dot_nn(e, rows[:, cols(f)])
        gy = (sy * (back - x[4, :, cols(f)].astype(F32) * sm)).astype(BF16)
        g[:, cols(f)] = gy
        return acc + dot_nn(gy, w[3, 1, cols(f), :])

    ga = lax.fori_loop(0, D // TILE, head, zero)

    def keep_or_send(k):
        return remote(fb.at[k], r1.at[k // 2], fs.at[k // 2], fr.at[k // 2], partner)

    def source(hh, q):
        return fb.at[2 * hh + c, :, :, q], fb.at[2 * hh + c, :, :, :, q]

    def stage_one(hh, i, view):
        return remote(view, r2.at[hh, i - 1], s1s.at[hh, i], s1r.at[hh, i], a_peers[i])

    def open_sum(hh):
        k = 2 * hh + c
        remote(fb.at[k], r1.at[hh], fs.at[hh], fr.at[hh], partner).wait_recv()

        def add(q, _):
            m, rest = q // 8, q % 8
            a, b = rest // 4, rest % 4
            fb[k, m, a, b] = (fb[k, m, a, b].astype(F32) + r1[hh, m, a, b].astype(F32)).astype(BF16)
            return 0

        lax.fori_loop(0, 16, add, 0)

        @pl.when(c == 0)
        def _():
            for i in range(1, 4):
                stage_one(hh, i, fb.at[k, :, :, (u + i) % 4]).start()

        @pl.when(c == 1)
        def _():
            for i in range(1, 4):
                stage_one(hh, i, fb.at[k, :, :, :, (u + i) % 4]).start()

    def stage_two(hh, i):
        return remote(
            s2.at[hh, :, :, (v + i) % 4], r3.at[hh, i - 1], s2s.at[hh, i], s2r.at[hh, i], b_peers[i]
        )

    def middle_sum(hh):
        k = 2 * hh + c
        for i in range(1, 4):
            stage_one(hh, i, r2.at[hh, i - 1]).wait_recv()

        def add_with(load):
            def add(q, _):
                m, rest = q // 8, q % 8
                a, b = rest // 4, rest % 4
                value = load(m, a, b).astype(F32)
                for i in range(3):
                    value = value + r2[hh, i, m, a, b].astype(F32)
                s2[hh, m, a, b] = value.astype(BF16)
                return 0

            lax.fori_loop(0, 16, add, 0)

        @pl.when(c == 0)
        def _():
            add_with(lambda m, a, b: fb[k, m, a, u, b])

        @pl.when(c == 1)
        def _():
            add_with(lambda m, a, b: fb[k, m, a, b, u])

        for i in range(1, 4):
            stage_two(hh, i).start()

    def last_sum(hh):
        for i in range(1, 4):
            stage_two(hh, i).wait_recv()
        for m in range(2):
            for a in range(2):
                value = s2[hh, m, a, v].astype(F32)
                for i in range(3):
                    value = value + r3[hh, i, m, a].astype(F32)
                s3[hh, a, m] = value.astype(BF16)

    for k in (3, 2, 1, 0):
        hk = hid[k]
        sk = scale[k][:, 0:1]
        gh = (ga * gelu_slope(hk)).astype(BF16)
        ghf = gh.astype(F32)
        mean = jnp.sum(ghf * hk, axis=1, keepdims=True) * (1.0 / D)
        gh2 = (ghf * ghf).astype(BF16)
        af = act[k].astype(F32)
        a2 = (af * af).astype(BF16)

        def step(f, acc, k=k, gh=gh, sk=sk, mean=mean):
            nf = x[k, :, cols(f)].astype(F32) * sk
            gf = g[:, cols(f)].astype(F32)
            n2[:, cols(f)] = (nf * nf).astype(BF16)
            g2[:, cols(f)] = (gf * gf).astype(BF16)
            if k == 0:
                return acc
            back = dot_nt(gh, w[k, 0, cols(f), :])
            gy = (gf + sk * (back - nf * mean)).astype(BF16)
            g[:, cols(f)] = gy
            return acc + dot_nn(gy, w[k - 1, 1, cols(f), :])

        ga = lax.fori_loop(0, D // TILE, step, zero)

        def outer(b, _, k=k, gh2=gh2, a2=a2):
            a = b // 2
            half = pl.ds((b % 2) * 2, 2)
            fd = dot_tn(n2[:, cols(b, BLK)], gh2).astype(BF16)
            fb[k, 0, a, half] = fd.reshape(2, 4, 144, 128)
            fu = dot_tn(g2[:, cols(b, BLK)], a2).astype(BF16)
            fb[k, 1, a, half] = fu.reshape(2, 4, 144, 128)
            return 0

        lax.fori_loop(0, 4, outer, 0)

        @pl.when(c != k % 2)
        def _(k=k):
            keep_or_send(k).start()

        if k == 2:

            @pl.when(c == 1)
            def _():
                open_sum(1)

        if k == 1:

            @pl.when(c == 0)
            def _():
                open_sum(1)

    open_sum(0)
    middle_sum(1)
    last_sum(1)
    middle_sum(0)
    last_sum(0)

    y_sends = []
    for i in range(1, 4):
        y_ = (y + i) % 4
        copy = remote(s3.at[y_ // 2, y_ % 2], r4.at[i], ys.at[i], yr.at[i], y_peers[i])
        copy.start()
        y_sends.append(copy)
    r4[0] = s3[h, yl]
    for copy in y_sends:
        copy.wait()
    den = jnp.zeros((2, 144, 128), F32)
    num = jnp.zeros((2, 144, 128), F32)
    for i in range(4):
        t = (y + 4 - i) % 4
        value = r4[i].astype(F32)
        den = den + value
        num = num + value * wd[t].astype(F32)
    den = den + merge_eps
    flog_out[...] = jnp.log(den)
    merged[:, yl, xx, zz] = (num / den).astype(BF16)

    neighbour = at(h, c, 1 - yl, xx, zz)
    near = remote(merged.at[:, yl, xx, zz], merged.at[:, yl, xx, zz], gs.at[0], gr.at[0], neighbour)
    near.start()
    near.wait()

    def two(u_, v_):
        return merged.at[:, :, u_ * (1 - c) + v_ * c, v_ * (1 - c) + u_ * c]

    g_sends = []
    for i in range(1, 4):
        copy = remote(two(u, v), two(u, v), gs.at[i], gr.at[i], a_peers[i])
        copy.start()
        g_sends.append(copy)
    for i in range(4):
        from_u = (u + 4 - i) % 4
        if i:
            remote(two(from_u, v), two(from_u, v), gs.at[i], gr.at[i], a_peers[i]).wait_recv()
        for j in range(1, 4):
            copy = remote(two(from_u, v), two(from_u, v), gs.at[4 * j + i], gr.at[4 * j + i], b_peers[j])
            copy.start()
            g_sends.append(copy)
    for i in range(4):
        from_u = (u + 4 - i) % 4
        for j in range(1, 4):
            from_v = (v + 4 - j) % 4
            remote(two(from_u, from_v), two(from_u, from_v), gs.at[4 * j + i], gr.at[4 * j + i], b_peers[j]).wait_recv()
    for copy in g_sends:
        copy.wait_send()

    to_next = remote(eval_out, vin, vs.at[0], vr.at[0], partner)
    to_after = remote(eval_out, vin, vs.at[0], vr.at[0], after)

    @pl.when(s == 0)
    def _():
        eval_load.wait()

    @pl.when(s != 0)
    def _():
        to_next.wait_recv()

    def weights(m, b):
        return merged[m, b // 2, pl.ds((b % 2) * 2, 2)].reshape(BLK, 128)

    small = jnp.zeros((ROWS, 128), F32)

    def eval_in(b, carry):
        total, acc = carry
        vt = vin[:, cols(b, BLK)]
        vf = vt.astype(F32)
        return total + lane_fold(vf * vf), acc + dot_nn(vt, weights(0, b))

    total, acc = lax.fori_loop(0, 4, eval_in, (small, small))
    sv = lax.rsqrt(jnp.sum(total, axis=1, keepdims=True) * (1.0 / D) + norm_eps)
    av = gelu_value(sv * acc).astype(BF16)

    def eval_step(b, _):
        eval_out[:, cols(b, BLK)] = (
            vin[:, cols(b, BLK)].astype(F32) + dot_nt(av, weights(1, b))
        ).astype(BF16)
        return 0

    lax.fori_loop(0, 4, eval_step, 0)

    @pl.when((s == 0) | (s == 2))
    def _():
        to_next.start()
        to_next.wait_send()

    @pl.when(s == 1)
    def _():
        to_after.start()
        to_after.wait_send()

    for hh in range(2):

        @pl.when(c == 1)
        def _(hh=hh):
            keep_or_send(2 * hh).wait_send()

        @pl.when(c == 0)
        def _(hh=hh):
            keep_or_send(2 * hh + 1).wait_send()

        for i in range(1, 4):
            stage_one(hh, i, r2.at[hh, i - 1]).wait_send()
            stage_two(hh, i).wait_send()

    @pl.when(c != yl)
    def _():
        give.wait()

    @pl.when(c == yl)
    def _():
        hold.wait()


def local(entry_states, down_proj, up_proj, label_rows, sampled_labels, eval_states):
    vmem = pl.BlockSpec(memory_space=pltpu.VMEM)
    hbm = pl.BlockSpec(memory_space=pl.ANY)
    dma = pltpu.SemaphoreType.DMA
    labels = jnp.broadcast_to(sampled_labels.reshape(TASKS, N, 1), (TASKS, N, 128))
    eval_out, logp, flog = pl.pallas_call(
        kernel,
        out_shape=(
            jax.ShapeDtypeStruct((ROWS, D), BF16),
            jax.ShapeDtypeStruct((N, 128), F32),
            jax.ShapeDtypeStruct((2, 144, 128), F32),
        ),
        in_specs=[hbm] * 6,
        out_specs=(vmem, vmem, vmem),
        scratch_shapes=[
            pltpu.VMEM((4, 2, D, R), BF16),
            pltpu.VMEM((5, N, D), BF16),
            pltpu.VMEM((N, D), BF16),
            pltpu.VMEM((LABELS, D), BF16),
            pltpu.VMEM((N, 128), jnp.int32),
            pltpu.VMEM((N, D), BF16),
            pltpu.VMEM((N, D), BF16),
            pltpu.VMEM((4, N, R), F32),
            pltpu.VMEM((4, N, R), BF16),
            pltpu.VMEM((4, N, 128), F32),
            pltpu.VMEM((4, 2, 2, 4, 4, 144, 128), BF16),
            pltpu.VMEM((2, 2, 2, 4, 4, 144, 128), BF16),
            pltpu.VMEM((2, 3, 2, 2, 4, 144, 128), BF16),
            pltpu.VMEM((2, 2, 2, 4, 144, 128), BF16),
            pltpu.VMEM((2, 3, 2, 2, 144, 128), BF16),
            pltpu.VMEM((2, 2, 2, 144, 128), BF16),
            pltpu.VMEM((4, 2, 144, 128), BF16),
            pltpu.VMEM((4, 2, 144, 128), BF16),
            pltpu.VMEM((2, 2, 4, 4, 144, 128), BF16),
            pltpu.VMEM((ROWS, D), BF16),
            pltpu.VMEM((N, 128), F32),
            dma((16,)),
            dma((2,)), dma((2,)),
            dma((2,)), dma((2,)),
            dma((4,)), dma((4,)),
            dma((4, 4)), dma((4, 4)),
            dma((4,)), dma((4,)),
            dma((3,)), dma((3,)),
            dma((2,)), dma((2,)),
            dma((2, 4)), dma((2, 4)),
            dma((2, 4)), dma((2, 4)),
            dma((4,)), dma((4,)),
            dma((16,)), dma((16,)),
            dma((1,)), dma((1,)),
        ],
        compiler_params=pltpu.CompilerParams(
            collective_id=0, has_side_effects=True, vmem_limit_bytes=67043328
        ),
        name="merge",
    )(
        down_proj.reshape(TASKS, D, R),
        up_proj.reshape(TASKS, D, R),
        entry_states.reshape(N, D),
        labels,
        label_rows,
        eval_states,
    )
    return (
        eval_out[None],
        logp[:, 0].reshape(1, MICRO, ROWS),
        flog[None],
    )


def solution(mesh):
    placed = (
        P(None, "dp", None),
        P("section", None, None, None),
        P("section", None, None, None),
        P(),
        P(None, None, "dp"),
        P("dp", None),
    )
    return jax.shard_map(
        local,
        mesh=mesh,
        in_specs=placed,
        out_specs=(
            P("section", "dp", None),
            P("section", None, "dp"),
            P("section", None, "dp", None),
        ),
        check_vma=False,
    )
```

```python
import jax
import jax.numpy as jnp
from jax import lax
from jax.experimental import pallas as pl
from jax.experimental.pallas import tpu as pltpu
from jax.sharding import PartitionSpec as P

norm_eps = 1e-06
merge_eps = 1e-06
soft_cap = 30.0
gelu_coef = 0.7978845608028654

D = 4608
R = 128
LABELS = 256
TASKS = 4
MICRO = 5
ROWS = 32
N = MICRO * ROWS
TILE = 512
BLK = D // 4
F32 = jnp.float32
BF16 = jnp.bfloat16
MESH = pl.DeviceIdType.MESH


def gelu_value(hidden):
    inner = gelu_coef * (hidden + 0.044715 * hidden * hidden * hidden)
    return 0.5 * hidden * (1.0 + jnp.tanh(inner))


def gelu_slope(hidden):
    inner = gelu_coef * (hidden + 0.044715 * hidden * hidden * hidden)
    t = jnp.tanh(inner)
    return 0.5 * (1.0 + t) + 0.5 * hidden * (1.0 - t * t) * gelu_coef * (
        1.0 + 3.0 * 0.044715 * hidden * hidden
    )


def dot_nn(a, b):
    return lax.dot_general(a, b, (((1,), (0,)), ((), ())), preferred_element_type=F32)


def dot_nt(a, b):
    return lax.dot_general(a, b, (((1,), (1,)), ((), ())), preferred_element_type=F32)


def dot_tn(a, b):
    return lax.dot_general(a, b, (((0,), (0,)), ((), ())), preferred_element_type=F32)


def over(count, body, carry):
    for i in range(count):
        carry = body(i, carry)
    return carry


def lane_fold(v):
    total = v[:, 0:128]
    for i in range(1, v.shape[1] // 128):
        total = total + v[:, i * 128 : (i + 1) * 128]
    return total


def kernel(
    down, up, entry, labels, label_rows, evals,
    eval_out, logp_out, flog_out,
    w, x, g, rows, lab, wide, narrow, hid, act, scale,
    fb, r1, r2, s2, r3, s3, r4, wd, merged, vin, picked,
    load_sem, ps, pr, cs, cr, as_, ar, bs, br, os_, orr, es, er, fs, fr,
    s1s, s1r, s2s, s2r, ys, yr, gs, gr, vs, vr,
):
    s = lax.axis_index("section")
    d = lax.axis_index("dp")
    h = s // 2
    c = s % 2
    yl = d // 16
    xx = (d // 4) % 4
    zz = d % 4
    y = 2 * h + yl
    u = xx * (1 - c) + zz * c
    v = zz * (1 - c) + xx * c

    def at(h_, c_, yl_, x_, z_):
        return {"section": h_ * 2 + c_, "dp": yl_ * 16 + x_ * 4 + z_}

    def at_uv(u_, v_):
        return at(h, c, yl, u_ * (1 - c) + v_ * c, v_ * (1 - c) + u_ * c)

    def at_y(y_, core=None):
        return at(y_ // 2, c if core is None else core, y_ % 2, xx, zz)

    partner = at(h, 1 - c, yl, xx, zz)
    swap = at(h, 1 - c, 1 - yl, xx, zz)
    across = at(1 - h, c, 1 - yl, xx, zz)
    after = at(1 - h, 1 - c, yl, xx, zz)
    third = at(1 - h, 1 - c, 1 - yl, xx, zz)
    a_peers = [None] + [at_uv((u + i) % 4, v) for i in range(1, 4)]
    b_peers = [None] + [at_uv(u, (v + i) % 4) for i in range(1, 4)]
    y_peers = [None] + [at_y((y + i) % 4) for i in range(1, 4)]

    def remote(src, dst, send, recv, to):
        return pltpu.make_async_remote_copy(
            src_ref=src, dst_ref=dst, send_sem=send, recv_sem=recv, device_id=to, device_id_type=MESH
        )

    barrier = pltpu.get_barrier_semaphore()
    everyone = [partner, swap, after, third] + a_peers[1:] + b_peers[1:] + y_peers[1:]
    for peer in everyone:
        pl.semaphore_signal(barrier, inc=1, device_id=peer, device_id_type=MESH)
    pl.semaphore_wait(barrier, len(everyone))

    far = 3 - y
    own = u * 4 + v
    part = D // 16
    slice_rows = pl.ds(own * part, part)
    cross = [
        remote(down.at[far, slice_rows], w.at[s, 0, slice_rows], cs.at[0], cr.at[0], across),
        remote(up.at[far, slice_rows], w.at[s, 1, slice_rows], cs.at[1], cr.at[1], across),
    ]
    for copy in cross:
        copy.start()
    beside = [
        remote(down.at[y], w.at[s, 0], ps.at[0], pr.at[0], partner),
        remote(up.at[y], w.at[s, 1], ps.at[1], pr.at[1], partner),
    ]
    moved = [
        remote(entry, x.at[0], es.at[0], er.at[0], swap),
        remote(labels.at[2 * h + 1 - yl], lab, es.at[1], er.at[1], swap),
    ]
    kept = [
        pltpu.make_async_copy(entry, x.at[0], load_sem.at[0]),
        pltpu.make_async_copy(labels.at[y], lab, load_sem.at[1]),
    ]

    @pl.when(c != yl)
    def _():
        for copy in moved:
            copy.start()

    @pl.when(c == yl)
    def _():
        for copy in kept:
            copy.start()

    for copy in beside:
        copy.start()
    loads = [
        pltpu.make_async_copy(down.at[y], w.at[s, 0], load_sem.at[2]),
        pltpu.make_async_copy(up.at[y], w.at[s, 1], load_sem.at[3]),
        pltpu.make_async_copy(label_rows, rows, load_sem.at[4]),
    ]
    mine = pl.ds(pl.multiple_of(d * 144, 16), 144)
    for t in range(TASKS):
        loads.append(pltpu.make_async_copy(down.at[t, mine], wd.at[t, 0], load_sem.at[5 + 2 * t]))
        loads.append(pltpu.make_async_copy(up.at[t, mine], wd.at[t, 1], load_sem.at[6 + 2 * t]))
    for copy in loads:
        copy.start()
    eval_load = pltpu.make_async_copy(evals, vin, load_sem.at[13])

    @pl.when(s == 0)
    def _():
        eval_load.start()

    lr = 2 * (1 - h) + c

    def piece(u_, v_):
        return w.at[lr, :, pl.ds((u_ * 4 + v_) * part, part)]

    for copy in cross:
        copy.wait_recv()
    a_sends = []
    for i in range(1, 4):
        copy = remote(piece(u, v), piece(u, v), as_.at[i], ar.at[i], a_peers[i])
        copy.start()
        a_sends.append(copy)
    b_sends = []
    for i in range(4):
        if i:
            from_u = (u + 4 - i) % 4
            remote(piece(from_u, v), piece(from_u, v), as_.at[i], ar.at[i], a_peers[i]).wait_recv()
        else:
            from_u = u
        for j in range(1, 4):
            copy = remote(piece(from_u, v), piece(from_u, v), bs.at[i, j], br.at[i, j], b_peers[j])
            copy.start()
            b_sends.append(copy)
    o_sends = []
    for i in range(4):
        from_u = (u + 4 - i) % 4
        for j in range(1, 4):
            from_v = (v + 4 - j) % 4
            remote(piece(from_u, from_v), piece(from_u, from_v), bs.at[i, j], br.at[i, j], b_peers[j]).wait_recv()
        block = w.at[lr, :, pl.ds(from_u * BLK, BLK)]
        copy = remote(block, block, os_.at[i], orr.at[i], partner)
        copy.start()
        o_sends.append(copy)

    @pl.when(c != yl)
    def _():
        for copy in moved:
            copy.wait()

    @pl.when(c == yl)
    def _():
        for copy in kept:
            copy.wait()

    for copy in beside:
        copy.wait()
    for copy in loads:
        copy.wait()
    for copy in cross + a_sends + b_sends:
        copy.wait_send()
    for copy in o_sends:
        copy.wait()

    zero = jnp.zeros((N, 128), F32)

    def cols(f, size=TILE):
        return pl.ds(f * size, size)

    def first(f, carry):
        total, acc = carry
        xt = x[0, :, cols(f)]
        xf = xt.astype(F32)
        return total + lane_fold(xf * xf), acc + dot_nn(xt, w[0, 0, cols(f), :])

    total, acc = over(D // TILE, first, (zero, zero))
    for k in range(4):
        sk = lax.rsqrt(jnp.sum(total, axis=1, keepdims=True) * (1.0 / D) + norm_eps)
        hk = sk * acc
        scale[k] = jnp.broadcast_to(sk, (N, 128))
        hid[k] = hk
        ak = gelu_value(hk).astype(BF16)
        act[k] = ak

        def step(f, carry, k=k, ak=ak):
            total, acc = carry
            new = (x[k, :, cols(f)].astype(F32) + dot_nt(ak, w[k, 1, cols(f), :])).astype(BF16)
            x[k + 1, :, cols(f)] = new
            nf = new.astype(F32)
            if k < 3:
                more = dot_nn(new, w[k + 1, 0, cols(f), :])
            else:
                more = dot_nt(new, rows[:, cols(f)])
            return total + lane_fold(nf * nf), acc + more

        width = R if k < 3 else LABELS
        total, acc = over(D // TILE, step, (zero, jnp.zeros((N, width), F32)))

    sy = lax.rsqrt(jnp.sum(total, axis=1, keepdims=True) * (1.0 / D) + norm_eps)
    logits = sy * acc
    bent = jnp.tanh(logits * (1.0 / soft_cap))
    capped = soft_cap * bent
    logp = capped - jnp.log(jnp.sum(jnp.exp(capped), axis=1, keepdims=True))
    hot = lab[:, 0:1] == lax.broadcasted_iota(jnp.int32, (N, LABELS), 1)
    chosen = jnp.sum(jnp.where(hot, logp, 0.0), axis=1, keepdims=True)
    picked[...] = jnp.broadcast_to(chosen, (N, 128))
    give = remote(picked, logp_out, es.at[2], er.at[2], swap)
    hold = pltpu.make_async_copy(picked, logp_out, load_sem.at[14])

    @pl.when(c != yl)
    def _():
        give.start()

    @pl.when(c == yl)
    def _():
        hold.start()

    e = ((jnp.exp(logp) - jnp.where(hot, 1.0, 0.0)) * (1.0 - bent * bent)).astype(BF16)
    mean = jnp.sum(e.astype(F32) * logits, axis=1, keepdims=True) * (1.0 / D)
    sm = sy * mean

    def head(f, acc):
        back = dot_nn(e, rows[:, cols(f)])
        gy = (sy * (back - x[4, :, cols(f)].astype(F32) * sm)).astype(BF16)
        g[:, cols(f)] = gy
        return acc + dot_nn(gy, w[3, 1, cols(f), :])

    ga = over(D // TILE, head, zero)

    def give_half(k):
        return remote(fb.at[k, 1 - c], r1.at[k], fs.at[k], fr.at[k], partner)

    def stage_one(k, i, view):
        return remote(view, r2.at[k, i - 1], s1s.at[k, i], s1r.at[k, i], a_peers[i])

    def open_sum(k):
        remote(fb.at[k, c], r1.at[k], fs.at[k], fr.at[k], partner).wait_recv()
        for a in range(2):
            for b in range(4):
                fb[k, c, a, b] = (fb[k, c, a, b].astype(F32) + r1[k, a, b].astype(F32)).astype(BF16)

        @pl.when(c == 0)
        def _():
            for i in (2, 1, 3):
                stage_one(k, i, fb.at[k, 0, :, (u + i) % 4]).start()

        @pl.when(c == 1)
        def _():
            for i in (2, 1, 3):
                stage_one(k, i, fb.at[k, 1, :, :, (u + i) % 4]).start()

    def stage_two(k, i):
        return remote(s2.at[k, :, (v + i) % 4], r3.at[k, i - 1], s2s.at[k, i], s2r.at[k, i], b_peers[i])

    def middle_sum(k):
        for i in range(1, 4):
            stage_one(k, i, r2.at[k, i - 1]).wait_recv()

        def add_with(load):
            for a in range(2):
                for b in range(4):
                    value = load(a, b).astype(F32)
                    for i in range(3):
                        value = value + r2[k, i, a, b].astype(F32)
                    s2[k, a, b] = value.astype(BF16)

        @pl.when(c == 0)
        def _():
            add_with(lambda a, b: fb[k, 0, a, u, b])

        @pl.when(c == 1)
        def _():
            add_with(lambda a, b: fb[k, 1, a, b, u])

        for i in (2, 1, 3):
            stage_two(k, i).start()

    def last_sum(k):
        for i in range(1, 4):
            stage_two(k, i).wait_recv()
        for a in range(2):
            value = s2[k, a, v].astype(F32)
            for i in range(3):
                value = value + r3[k, i, a].astype(F32)
            s3[k, a] = value.astype(BF16)

    for k in (3, 2, 1, 0):
        hk = hid[k]
        sk = scale[k][:, 0:1]
        gh = (ga * gelu_slope(hk)).astype(BF16)
        ghf = gh.astype(F32)
        mean = jnp.sum(ghf * hk, axis=1, keepdims=True) * (1.0 / D)
        narrow[0] = (ghf * ghf).astype(BF16)
        af = act[k].astype(F32)
        narrow[1] = (af * af).astype(BF16)

        def step(f, acc, k=k, gh=gh, sk=sk, mean=mean):
            nf = x[k, :, cols(f)].astype(F32) * sk
            gf = g[:, cols(f)].astype(F32)
            wide[0, :, cols(f)] = (nf * nf).astype(BF16)
            wide[1, :, cols(f)] = (gf * gf).astype(BF16)
            if k == 0:
                return acc
            back = dot_nt(gh, w[k, 0, cols(f), :])
            gy = (gf + sk * (back - nf * mean)).astype(BF16)
            g[:, cols(f)] = gy
            return acc + dot_nn(gy, w[k - 1, 1, cols(f), :])

        ga = over(D // TILE, step, zero)
        if k < 3:
            open_sum(k + 1)
        for m in (1 - c, c):
            thin = narrow[m]
            for b in range(4):
                value = dot_tn(wide[m, :, cols(b, BLK)], thin).astype(BF16)
                fb[k, m, b // 2, pl.ds((b % 2) * 2, 2)] = value.reshape(2, 4, 144, 128)
            if m is not c:
                give_half(k).start()
        if k < 2:
            middle_sum(k + 2)

    open_sum(0)
    last_sum(3)
    middle_sum(1)
    last_sum(2)
    middle_sum(0)
    last_sum(1)
    last_sum(0)

    y_sends = []
    for i in range(4):
        y_ = (y + i) % 4
        for j in range(2):
            core = (c + j) % 2
            if i or j:
                copy = remote(
                    s3.at[2 * (y_ // 2) + core, y_ % 2], r4.at[i, c],
                    ys.at[i, j], yr.at[i, j], at_y(y_, core),
                )
                copy.start()
                y_sends.append(copy)
    r4[0, c] = s3[s, yl]
    for copy in y_sends:
        copy.wait()
    den = jnp.zeros((2, 144, 128), F32)
    num = jnp.zeros((2, 144, 128), F32)
    for i in range(4):
        t = (y + 4 - i) % 4
        value = r4[i].astype(F32)
        den = den + value
        num = num + value * wd[t].astype(F32)
    den = den + merge_eps
    flog_out[...] = jnp.log(den)
    merged[:, yl, xx, zz] = (num / den).astype(BF16)

    neighbour = at(h, c, 1 - yl, xx, zz)
    near = remote(merged.at[:, yl, xx, zz], merged.at[:, yl, xx, zz], gs.at[0], gr.at[0], neighbour)
    near.start()
    near.wait()

    def two(u_, v_):
        return merged.at[:, :, u_ * (1 - c) + v_ * c, v_ * (1 - c) + u_ * c]

    g_sends = []
    for i in range(1, 4):
        copy = remote(two(u, v), two(u, v), gs.at[i], gr.at[i], a_peers[i])
        copy.start()
        g_sends.append(copy)
    for i in range(4):
        from_u = (u + 4 - i) % 4
        if i:
            remote(two(from_u, v), two(from_u, v), gs.at[i], gr.at[i], a_peers[i]).wait_recv()
        for j in range(1, 4):
            copy = remote(two(from_u, v), two(from_u, v), gs.at[4 * j + i], gr.at[4 * j + i], b_peers[j])
            copy.start()
            g_sends.append(copy)
    for i in range(4):
        from_u = (u + 4 - i) % 4
        for j in range(1, 4):
            from_v = (v + 4 - j) % 4
            remote(two(from_u, from_v), two(from_u, from_v), gs.at[4 * j + i], gr.at[4 * j + i], b_peers[j]).wait_recv()
    for copy in g_sends:
        copy.wait_send()

    def hand_on(b, to):
        return remote(eval_out.at[:, cols(b, BLK)], vin.at[:, cols(b, BLK)], vs.at[b], vr.at[b], to)

    @pl.when(s == 0)
    def _():
        eval_load.wait()

    def weights(m, b):
        return merged[m, b // 2, pl.ds((b % 2) * 2, 2)].reshape(BLK, 128)

    total = jnp.zeros((ROWS, 128), F32)
    acc = jnp.zeros((ROWS, 128), F32)
    for b in range(4):

        @pl.when(s != 0)
        def _(b=b):
            hand_on(b, partner).wait_recv()

        vt = vin[:, cols(b, BLK)]
        vf = vt.astype(F32)
        total = total + lane_fold(vf * vf)
        acc = acc + dot_nn(vt, weights(0, b))
    sv = lax.rsqrt(jnp.sum(total, axis=1, keepdims=True) * (1.0 / D) + norm_eps)
    av = gelu_value(sv * acc).astype(BF16)
    for b in range(4):
        eval_out[:, cols(b, BLK)] = (
            vin[:, cols(b, BLK)].astype(F32) + dot_nt(av, weights(1, b))
        ).astype(BF16)

        @pl.when(c == 0)
        def _(b=b):
            hand_on(b, partner).start()

        @pl.when(s == 1)
        def _(b=b):
            hand_on(b, after).start()

    for b in range(4):

        @pl.when(s != 3)
        def _(b=b):
            hand_on(b, partner).wait_send()

    for k in range(4):
        give_half(k).wait_send()
        for i in range(1, 4):
            stage_one(k, i, r2.at[k, i - 1]).wait_send()
            stage_two(k, i).wait_send()

    @pl.when(c != yl)
    def _():
        give.wait()

    @pl.when(c == yl)
    def _():
        hold.wait()


def local(entry_states, down_proj, up_proj, label_rows, sampled_labels, eval_states):
    vmem = pl.BlockSpec(memory_space=pltpu.VMEM)
    hbm = pl.BlockSpec(memory_space=pl.ANY)
    dma = pltpu.SemaphoreType.DMA
    labels = jnp.broadcast_to(sampled_labels.reshape(TASKS, N, 1), (TASKS, N, 128))
    eval_out, logp, flog = pl.pallas_call(
        kernel,
        out_shape=(
            jax.ShapeDtypeStruct((ROWS, D), BF16),
            jax.ShapeDtypeStruct((N, 128), F32),
            jax.ShapeDtypeStruct((2, 144, 128), F32),
        ),
        in_specs=[hbm] * 6,
        out_specs=(vmem, vmem, vmem),
        scratch_shapes=[
            pltpu.VMEM((4, 2, D, R), BF16),
            pltpu.VMEM((5, N, D), BF16),
            pltpu.VMEM((N, D), BF16),
            pltpu.VMEM((LABELS, D), BF16),
            pltpu.VMEM((N, 128), jnp.int32),
            pltpu.VMEM((2, N, D), BF16),
            pltpu.VMEM((2, N, R), BF16),
            pltpu.VMEM((4, N, R), F32),
            pltpu.VMEM((4, N, R), BF16),
            pltpu.VMEM((4, N, 128), F32),
            pltpu.VMEM((4, 2, 2, 4, 4, 144, 128), BF16),
            pltpu.VMEM((4, 2, 4, 4, 144, 128), BF16),
            pltpu.VMEM((4, 3, 2, 4, 144, 128), BF16),
            pltpu.VMEM((4, 2, 4, 144, 128), BF16),
            pltpu.VMEM((4, 3, 2, 144, 128), BF16),
            pltpu.VMEM((4, 2, 144, 128), BF16),
            pltpu.VMEM((4, 2, 144, 128), BF16),
            pltpu.VMEM((4, 2, 144, 128), BF16),
            pltpu.VMEM((2, 2, 4, 4, 144, 128), BF16),
            pltpu.VMEM((ROWS, D), BF16),
            pltpu.VMEM((N, 128), F32),
            dma((16,)),
            dma((2,)), dma((2,)),
            dma((2,)), dma((2,)),
            dma((4,)), dma((4,)),
            dma((4, 4)), dma((4, 4)),
            dma((4,)), dma((4,)),
            dma((3,)), dma((3,)),
            dma((4,)), dma((4,)),
            dma((4, 4)), dma((4, 4)),
            dma((4, 4)), dma((4, 4)),
            dma((4, 2)), dma((4, 2)),
            dma((16,)), dma((16,)),
            dma((4,)), dma((4,)),
        ],
        compiler_params=pltpu.CompilerParams(
            collective_id=0, has_side_effects=True, vmem_limit_bytes=67043328
        ),
        name="merge",
    )(
        down_proj.reshape(TASKS, D, R),
        up_proj.reshape(TASKS, D, R),
        entry_states.reshape(N, D),
        labels,
        label_rows,
        eval_states,
    )
    return (
        eval_out[None],
        logp[:, 0].reshape(1, MICRO, ROWS),
        flog[None],
    )


def solution(mesh):
    placed = (
        P(None, "dp", None),
        P("section", None, None, None),
        P("section", None, None, None),
        P(),
        P(None, None, "dp"),
        P("dp", None),
    )
    return jax.shard_map(
        local,
        mesh=mesh,
        in_specs=placed,
        out_specs=(
            P("section", "dp", None),
            P("section", None, "dp"),
            P("section", None, "dp", None),
        ),
        check_vma=False,
    )
```

```python
import jax
import jax.numpy as jnp
from jax import lax
from jax.experimental import pallas as pl
from jax.experimental.pallas import tpu as pltpu
from jax.sharding import PartitionSpec as P

norm_eps = 1e-06
merge_eps = 1e-06
soft_cap = 30.0
gelu_coef = 0.7978845608028654

D = 4608
R = 128
LABELS = 256
TASKS = 4
MICRO = 5
ROWS = 32
N = MICRO * ROWS
TILE = 512
BLK = D // 4
F32 = jnp.float32
BF16 = jnp.bfloat16
MESH = pl.DeviceIdType.MESH


def gelu_value(hidden):
    inner = gelu_coef * (hidden + 0.044715 * hidden * hidden * hidden)
    return 0.5 * hidden * (1.0 + jnp.tanh(inner))


def gelu_slope(hidden):
    inner = gelu_coef * (hidden + 0.044715 * hidden * hidden * hidden)
    t = jnp.tanh(inner)
    return 0.5 * (1.0 + t) + 0.5 * hidden * (1.0 - t * t) * gelu_coef * (
        1.0 + 3.0 * 0.044715 * hidden * hidden
    )


def dot_nn(a, b):
    return lax.dot_general(a, b, (((1,), (0,)), ((), ())), preferred_element_type=F32)


def dot_nt(a, b):
    return lax.dot_general(a, b, (((1,), (1,)), ((), ())), preferred_element_type=F32)


def dot_tn(a, b):
    return lax.dot_general(a, b, (((0,), (0,)), ((), ())), preferred_element_type=F32)


def over(count, body, carry):
    for i in range(count):
        carry = body(i, carry)
    return carry


def lane_fold(v):
    total = v[:, 0:128]
    for i in range(1, v.shape[1] // 128):
        total = total + v[:, i * 128 : (i + 1) * 128]
    return total


def kernel(
    down, up, entry, labels, label_rows, evals,
    eval_out, logp_out, flog_out,
    w, x, g, rows, lab, wide, narrow, hid, act, scale,
    fb, r1, r2, s2, r3, s3, r4, dens, wd, merged, vin, picked,
    load_sem, ps, pr, cs, cr, as_, ar, bs, br, os_, orr, es, er, fs, fr,
    s1s, s1r, s2s, s2r, ys, yr, gas, gar, gbs, gbr, vs, vr,
):
    s = lax.axis_index("section")
    d = lax.axis_index("dp")
    h = s // 2
    c = s % 2
    yl = d // 16
    xx = (d // 4) % 4
    zz = d % 4
    y = 2 * h + yl
    u = xx * (1 - c) + zz * c
    v = zz * (1 - c) + xx * c

    def at(h_, c_, yl_, x_, z_):
        return {"section": h_ * 2 + c_, "dp": yl_ * 16 + x_ * 4 + z_}

    def at_uv(u_, v_):
        return at(h, c, yl, u_ * (1 - c) + v_ * c, v_ * (1 - c) + u_ * c)

    def at_y(y_, core=None):
        return at(y_ // 2, c if core is None else core, y_ % 2, xx, zz)

    partner = at(h, 1 - c, yl, xx, zz)
    swap = at(h, 1 - c, 1 - yl, xx, zz)
    across = at(1 - h, c, 1 - yl, xx, zz)
    after = at(1 - h, 1 - c, yl, xx, zz)
    third = at(1 - h, 1 - c, 1 - yl, xx, zz)
    a_peers = [None] + [at_uv((u + i) % 4, v) for i in range(1, 4)]
    b_peers = [None] + [at_uv(u, (v + i) % 4) for i in range(1, 4)]
    x_peers = [None] + [at(h, c, yl, (xx + i) % 4, zz) for i in range(1, 4)]
    z_peers = [None] + [at(h, c, yl, xx, (zz + i) % 4) for i in range(1, 4)]
    y_peers = [None] + [at_y((y + i) % 4) for i in range(1, 4)]

    def remote(src, dst, send, recv, to):
        return pltpu.make_async_remote_copy(
            src_ref=src, dst_ref=dst, send_sem=send, recv_sem=recv, device_id=to, device_id_type=MESH
        )

    barrier = pltpu.get_barrier_semaphore()
    everyone = [partner, swap, after, third] + a_peers[1:] + b_peers[1:] + y_peers[1:]
    for peer in everyone:
        pl.semaphore_signal(barrier, inc=1, device_id=peer, device_id_type=MESH)
    pl.semaphore_wait(barrier, len(everyone))

    far = 3 - y
    own = u * 4 + v
    part = D // 16
    slice_rows = pl.ds(own * part, part)
    cross = [
        remote(down.at[far, slice_rows], w.at[s, 0, slice_rows], cs.at[0], cr.at[0], across),
        remote(up.at[far, slice_rows], w.at[s, 1, slice_rows], cs.at[1], cr.at[1], across),
    ]
    for copy in cross:
        copy.start()
    beside = [
        remote(down.at[y], w.at[s, 0], ps.at[0], pr.at[0], partner),
        remote(up.at[y], w.at[s, 1], ps.at[1], pr.at[1], partner),
    ]
    moved = [
        remote(entry, x.at[0], es.at[0], er.at[0], swap),
        remote(labels.at[2 * h + 1 - yl], lab, es.at[1], er.at[1], swap),
    ]
    kept = [
        pltpu.make_async_copy(entry, x.at[0], load_sem.at[0]),
        pltpu.make_async_copy(labels.at[y], lab, load_sem.at[1]),
    ]

    @pl.when(c != yl)
    def _():
        for copy in moved:
            copy.start()

    @pl.when(c == yl)
    def _():
        for copy in kept:
            copy.start()

    for copy in beside:
        copy.start()
    loads = [
        pltpu.make_async_copy(down.at[y], w.at[s, 0], load_sem.at[2]),
        pltpu.make_async_copy(up.at[y], w.at[s, 1], load_sem.at[3]),
        pltpu.make_async_copy(label_rows, rows, load_sem.at[4]),
    ]
    for t in range(TASKS):
        for a in range(2):
            mine = pl.ds(pl.multiple_of((a * 16 + xx * 4 + zz) * 144, 16), 144)
            for m, whole in enumerate((down, up)):
                sem = load_sem.at[16 + 4 * t + 2 * a + m]
                loads.append(pltpu.make_async_copy(whole.at[t, mine], wd.at[t, m, a], sem))
    for copy in loads:
        copy.start()
    eval_load = pltpu.make_async_copy(evals, vin, load_sem.at[13])

    @pl.when(s == 0)
    def _():
        eval_load.start()

    lr = 2 * (1 - h) + c

    def piece(u_, v_):
        return w.at[lr, :, pl.ds((u_ * 4 + v_) * part, part)]

    for copy in cross:
        copy.wait_recv()
    a_sends = []
    for i in range(1, 4):
        copy = remote(piece(u, v), piece(u, v), as_.at[i], ar.at[i], a_peers[i])
        copy.start()
        a_sends.append(copy)
    b_sends = []
    for i in range(4):
        if i:
            from_u = (u + 4 - i) % 4
            remote(piece(from_u, v), piece(from_u, v), as_.at[i], ar.at[i], a_peers[i]).wait_recv()
        else:
            from_u = u
        for j in range(1, 4):
            copy = remote(piece(from_u, v), piece(from_u, v), bs.at[i, j], br.at[i, j], b_peers[j])
            copy.start()
            b_sends.append(copy)
    o_sends = []
    for i in range(4):
        from_u = (u + 4 - i) % 4
        for j in range(1, 4):
            from_v = (v + 4 - j) % 4
            remote(piece(from_u, from_v), piece(from_u, from_v), bs.at[i, j], br.at[i, j], b_peers[j]).wait_recv()
        block = w.at[lr, :, pl.ds(from_u * BLK, BLK)]
        copy = remote(block, block, os_.at[i], orr.at[i], partner)
        copy.start()
        o_sends.append(copy)

    @pl.when(c != yl)
    def _():
        for copy in moved:
            copy.wait()

    @pl.when(c == yl)
    def _():
        for copy in kept:
            copy.wait()

    for copy in beside:
        copy.wait()
    for copy in loads:
        copy.wait()
    for copy in cross + a_sends + b_sends:
        copy.wait_send()
    for copy in o_sends:
        copy.wait()

    zero = jnp.zeros((N, 128), F32)

    def cols(f, size=TILE):
        return pl.ds(f * size, size)

    def first(f, carry):
        total, acc = carry
        xt = x[0, :, cols(f)]
        xf = xt.astype(F32)
        return total + lane_fold(xf * xf), acc + dot_nn(xt, w[0, 0, cols(f), :])

    total, acc = over(D // TILE, first, (zero, zero))
    for k in range(4):
        sk = lax.rsqrt(jnp.sum(total, axis=1, keepdims=True) * (1.0 / D) + norm_eps)
        hk = sk * acc
        scale[k] = jnp.broadcast_to(sk, (N, 128))
        hid[k] = hk
        ak = gelu_value(hk).astype(BF16)
        act[k] = ak

        def step(f, carry, k=k, ak=ak):
            total, acc = carry
            new = (x[k, :, cols(f)].astype(F32) + dot_nt(ak, w[k, 1, cols(f), :])).astype(BF16)
            x[k + 1, :, cols(f)] = new
            nf = new.astype(F32)
            if k < 3:
                more = dot_nn(new, w[k + 1, 0, cols(f), :])
            else:
                more = dot_nt(new, rows[:, cols(f)])
            return total + lane_fold(nf * nf), acc + more

        width = R if k < 3 else LABELS
        total, acc = over(D // TILE, step, (zero, jnp.zeros((N, width), F32)))

    sy = lax.rsqrt(jnp.sum(total, axis=1, keepdims=True) * (1.0 / D) + norm_eps)
    logits = sy * acc
    bent = jnp.tanh(logits * (1.0 / soft_cap))
    capped = soft_cap * bent
    logp = capped - jnp.log(jnp.sum(jnp.exp(capped), axis=1, keepdims=True))
    hot = lab[:, 0:1] == lax.broadcasted_iota(jnp.int32, (N, LABELS), 1)
    chosen = jnp.sum(jnp.where(hot, logp, 0.0), axis=1, keepdims=True)
    picked[...] = jnp.broadcast_to(chosen, (N, 128))
    give = remote(picked, logp_out, es.at[2], er.at[2], swap)
    hold = pltpu.make_async_copy(picked, logp_out, load_sem.at[14])

    @pl.when(c != yl)
    def _():
        give.start()

    @pl.when(c == yl)
    def _():
        hold.start()

    e = ((jnp.exp(logp) - jnp.where(hot, 1.0, 0.0)) * (1.0 - bent * bent)).astype(BF16)
    mean = jnp.sum(e.astype(F32) * logits, axis=1, keepdims=True) * (1.0 / D)
    sm = sy * mean

    def squares(k, f, gy):
        nf = x[k, :, cols(f)].astype(F32) * scale[k][:, 0:1]
        gf = gy.astype(F32)
        wide[0, :, cols(f)] = (nf * nf).astype(BF16)
        wide[1, :, cols(f)] = (gf * gf).astype(BF16)

    def head(f, acc):
        back = dot_nn(e, rows[:, cols(f)])
        gy = (sy * (back - x[4, :, cols(f)].astype(F32) * sm)).astype(BF16)
        g[:, cols(f)] = gy
        squares(3, f, gy)
        return acc + dot_nn(gy, w[3, 1, cols(f), :])

    ga = over(D // TILE, head, zero)

    def give_half(k):
        return remote(fb.at[k, 1 - c], r1.at[k], fs.at[k], fr.at[k], partner)

    def stage_one(k, i, view):
        return remote(view, r2.at[k, i - 1], s1s.at[k, i], s1r.at[k, i], a_peers[i])

    def open_sum(k):
        remote(fb.at[k, c], r1.at[k], fs.at[k], fr.at[k], partner).wait_recv()
        for a in range(2):
            for b in range(4):
                fb[k, c, a, b] = (fb[k, c, a, b].astype(F32) + r1[k, a, b].astype(F32)).astype(BF16)

        @pl.when(c == 0)
        def _():
            for i in (2, 1, 3):
                stage_one(k, i, fb.at[k, 0, :, (u + i) % 4]).start()

        @pl.when(c == 1)
        def _():
            for i in (2, 1, 3):
                stage_one(k, i, fb.at[k, 1, :, :, (u + i) % 4]).start()

    def stage_two(k, i):
        return remote(s2.at[k, :, (v + i) % 4], r3.at[k, i - 1], s2s.at[k, i], s2r.at[k, i], b_peers[i])

    def middle_sum(k):
        for i in range(1, 4):
            stage_one(k, i, r2.at[k, i - 1]).wait_recv()

        def add_with(load):
            for a in range(2):
                for b in range(4):
                    value = load(a, b).astype(F32)
                    for i in range(3):
                        value = value + r2[k, i, a, b].astype(F32)
                    s2[k, a, b] = value.astype(BF16)

        @pl.when(c == 0)
        def _():
            add_with(lambda a, b: fb[k, 0, a, u, b])

        @pl.when(c == 1)
        def _():
            add_with(lambda a, b: fb[k, 1, a, b, u])

        for i in (2, 1, 3):
            stage_two(k, i).start()

    def along_y(k, q):
        y_ = 2 * (k // 2) + q
        slot = (y_ + 4 - y) % 4
        return remote(s3.at[k], r4.at[slot, c], ys.at[k, q], yr.at[slot, c], at(k // 2, k % 2, q, xx, zz))

    def is_me(k, q):
        return (h == k // 2) & (c == k % 2) & (yl == q)

    def last_sum(k):
        for i in range(1, 4):
            stage_two(k, i).wait_recv()
        for a in range(2):
            value = s2[k, a, v].astype(F32)
            for i in range(3):
                value = value + r3[k, i, a].astype(F32)
            s3[k, a] = value.astype(BF16)
        for q in range(2):

            @pl.when(jnp.logical_not(is_me(k, q)))
            def _(q=q):
                along_y(k, q).start()

            @pl.when(is_me(k, q))
            def _():
                r4[0, c] = s3[k]

    def block(m, x_, z_):
        return merged.at[m, :, x_, z_]

    def gather_a(m, i):
        peers = (x_peers, z_peers)[m]
        return remote(block(m, xx, zz), block(m, xx, zz), gas.at[m, i], gar.at[m, i], peers[i])

    def gather_b(m, i, j):
        x_ = (xx + 4 - i) % 4 if m == 0 else xx
        z_ = (zz + 4 - i) % 4 if m == 1 else zz
        peers = (z_peers, x_peers)[m]
        return remote(block(m, x_, z_), block(m, x_, z_), gbs.at[m, i, j], gbr.at[m, i, j], peers[j])

    def merge():
        for i in range(4):
            for m in range(2):
                arrived = remote(r4.at[i, m], r4.at[i, m], ys.at[0, 0], yr.at[i, m], partner)
                if i:
                    arrived.wait_recv()
                else:

                    @pl.when(c != m)
                    def _(arrived=arrived):
                        arrived.wait_recv()

        for m in range(2):
            for a in range(2):
                den = jnp.zeros((144, 128), F32)
                num = jnp.zeros((144, 128), F32)
                for i in range(4):
                    t = (y + 4 - i) % 4
                    value = r4[i, m, a].astype(F32)
                    den = den + value
                    num = num + value * wd[t, m, a].astype(F32)
                den = den + merge_eps
                dens[a, m] = den
                merged[m, a, xx, zz] = (num / den).astype(BF16)
            for i in (1, 3, 2):
                gather_a(m, i).start()

    def pass_on():
        for i in (0, 1, 3, 2):
            for m in range(2):
                if i:
                    gather_a(m, i).wait_recv()
                for j in (1, 3, 2):
                    gather_b(m, i, j).start()

    for k in (3, 2, 1, 0):
        hk = hid[k]
        sk = scale[k][:, 0:1]
        gh = (ga * gelu_slope(hk)).astype(BF16)
        ghf = gh.astype(F32)
        mean = jnp.sum(ghf * hk, axis=1, keepdims=True) * (1.0 / D)
        narrow[0] = (ghf * ghf).astype(BF16)
        af = act[k].astype(F32)
        narrow[1] = (af * af).astype(BF16)

        for m in (1 - c, c):
            thin = narrow[m]
            for b in range(4):
                value = dot_tn(wide[m, :, cols(b, BLK)], thin).astype(BF16)
                fb[k, m, b // 2, pl.ds((b % 2) * 2, 2)] = value.reshape(2, 4, 144, 128)
            if m is not c:
                give_half(k).start()
        if k == 0:
            break

        def step(f, acc, k=k, gh=gh, sk=sk, sm=sk * mean):
            back = dot_nt(gh, w[k, 0, cols(f), :])
            gy = (
                g[:, cols(f)].astype(F32) + (sk * back - x[k, :, cols(f)].astype(F32) * (sk * sm))
            ).astype(BF16)
            g[:, cols(f)] = gy
            squares(k - 1, f, gy)
            return acc + dot_nn(gy, w[k - 1, 1, cols(f), :])

        ga = over(D // TILE, step, zero)
        open_sum(k)

    middle_sum(3)
    open_sum(0)
    last_sum(3)
    middle_sum(2)
    last_sum(2)
    middle_sum(1)
    last_sum(1)
    middle_sum(0)

    @pl.when(s != 0)
    def _():
        merge()

    last_sum(0)

    @pl.when(s == 0)
    def _():
        merge()

    pass_on()

    def hand_on(b, to):
        return remote(eval_out.at[:, cols(b, BLK)], vin.at[:, cols(b, BLK)], vs.at[b], vr.at[b], to)

    @pl.when(s == 0)
    def _():
        eval_load.wait()

    def weights(m, b):
        return merged[m, b // 2, pl.ds((b % 2) * 2, 2)].reshape(BLK, 128)

    for i in range(4):
        for j in range(1, 4):
            gather_b(0, i, j).wait_recv()
    total = jnp.zeros((ROWS, 128), F32)
    acc = jnp.zeros((ROWS, 128), F32)
    for b in range(4):

        @pl.when(s != 0)
        def _(b=b):
            hand_on(b, partner).wait_recv()

        vt = vin[:, cols(b, BLK)]
        vf = vt.astype(F32)
        total = total + lane_fold(vf * vf)
        acc = acc + dot_nn(vt, weights(0, b))
    sv = lax.rsqrt(jnp.sum(total, axis=1, keepdims=True) * (1.0 / D) + norm_eps)
    av = gelu_value(sv * acc).astype(BF16)
    for i in range(4):
        for j in range(1, 4):
            gather_b(1, i, j).wait_recv()
    for b in range(4):
        eval_out[:, cols(b, BLK)] = (
            vin[:, cols(b, BLK)].astype(F32) + dot_nt(av, weights(1, b))
        ).astype(BF16)

        @pl.when(c == 0)
        def _(b=b):
            hand_on(b, partner).start()

        @pl.when(s == 1)
        def _(b=b):
            hand_on(b, after).start()

    for m in range(2):
        flog_out[m] = jnp.log(dens[yl, m])
    for b in range(4):

        @pl.when(s != 3)
        def _(b=b):
            hand_on(b, partner).wait_send()

    for m in range(2):
        for j in range(1, 4):
            gather_a(m, j).wait_send()
            for i in range(4):
                gather_b(m, i, j).wait_send()
    for k in range(4):
        for q in range(2):

            @pl.when(jnp.logical_not(is_me(k, q)))
            def _(k=k, q=q):
                along_y(k, q).wait_send()

        give_half(k).wait_send()
        for i in range(1, 4):
            stage_one(k, i, r2.at[k, i - 1]).wait_send()
            stage_two(k, i).wait_send()

    @pl.when(c != yl)
    def _():
        give.wait()

    @pl.when(c == yl)
    def _():
        hold.wait()


def local(entry_states, down_proj, up_proj, label_rows, sampled_labels, eval_states):
    vmem = pl.BlockSpec(memory_space=pltpu.VMEM)
    hbm = pl.BlockSpec(memory_space=pl.ANY)
    dma = pltpu.SemaphoreType.DMA
    labels = jnp.broadcast_to(sampled_labels.reshape(TASKS, N, 1), (TASKS, N, 128))
    eval_out, logp, flog = pl.pallas_call(
        kernel,
        out_shape=(
            jax.ShapeDtypeStruct((ROWS, D), BF16),
            jax.ShapeDtypeStruct((N, 128), F32),
            jax.ShapeDtypeStruct((2, 144, 128), F32),
        ),
        in_specs=[hbm] * 6,
        out_specs=(vmem, vmem, vmem),
        scratch_shapes=[
            pltpu.VMEM((4, 2, D, R), BF16),
            pltpu.VMEM((5, N, D), BF16),
            pltpu.VMEM((N, D), BF16),
            pltpu.VMEM((LABELS, D), BF16),
            pltpu.VMEM((N, 128), jnp.int32),
            pltpu.VMEM((2, N, D), BF16),
            pltpu.VMEM((2, N, R), BF16),
            pltpu.VMEM((4, N, R), F32),
            pltpu.VMEM((4, N, R), BF16),
            pltpu.VMEM((4, N, 128), F32),
            pltpu.VMEM((4, 2, 2, 4, 4, 144, 128), BF16),
            pltpu.VMEM((4, 2, 4, 4, 144, 128), BF16),
            pltpu.VMEM((4, 3, 2, 4, 144, 128), BF16),
            pltpu.VMEM((4, 2, 4, 144, 128), BF16),
            pltpu.VMEM((4, 3, 2, 144, 128), BF16),
            pltpu.VMEM((4, 2, 144, 128), BF16),
            pltpu.VMEM((4, 2, 2, 144, 128), BF16),
            pltpu.VMEM((2, 2, 144, 128), F32),
            pltpu.VMEM((4, 2, 2, 144, 128), BF16),
            pltpu.VMEM((2, 2, 4, 4, 144, 128), BF16),
            pltpu.VMEM((ROWS, D), BF16),
            pltpu.VMEM((N, 128), F32),
            dma((32,)),
            dma((2,)), dma((2,)),
            dma((2,)), dma((2,)),
            dma((4,)), dma((4,)),
            dma((4, 4)), dma((4, 4)),
            dma((4,)), dma((4,)),
            dma((3,)), dma((3,)),
            dma((4,)), dma((4,)),
            dma((4, 4)), dma((4, 4)),
            dma((4, 4)), dma((4, 4)),
            dma((4, 2)), dma((4, 2)),
            dma((2, 4)), dma((2, 4)),
            dma((2, 4, 4)), dma((2, 4, 4)),
            dma((4,)), dma((4,)),
        ],
        compiler_params=pltpu.CompilerParams(
            collective_id=0, has_side_effects=True, vmem_limit_bytes=67043328
        ),
        name="merge",
    )(
        down_proj.reshape(TASKS, D, R),
        up_proj.reshape(TASKS, D, R),
        entry_states.reshape(N, D),
        labels,
        label_rows,
        eval_states,
    )
    return (
        eval_out[None],
        logp[:, 0].reshape(1, MICRO, ROWS),
        flog[None],
    )


def solution(mesh):
    placed = (
        P(None, "dp", None),
        P("section", None, None, None),
        P("section", None, None, None),
        P(),
        P(None, None, "dp"),
        P("dp", None),
    )
    return jax.shard_map(
        local,
        mesh=mesh,
        in_specs=placed,
        out_specs=(
            P("section", "dp", None),
            P("section", None, "dp"),
            P("section", None, "dp", None),
        ),
        check_vma=False,
    )
```

```python
import jax
import jax.numpy as jnp
from jax import lax
from jax.experimental import pallas as pl
from jax.experimental.pallas import tpu as pltpu
from jax.sharding import PartitionSpec as P

norm_eps = 1e-06
merge_eps = 1e-06
soft_cap = 30.0
gelu_coef = 0.7978845608028654

D = 4608
R = 128
LABELS = 256
TASKS = 4
MICRO = 5
ROWS = 32
N = MICRO * ROWS
TILE = 512
BLK = D // 4
F32 = jnp.float32
BF16 = jnp.bfloat16
MESH = pl.DeviceIdType.MESH


def gelu_value(hidden):
    inner = gelu_coef * (hidden + 0.044715 * hidden * hidden * hidden)
    return 0.5 * hidden * (1.0 + jnp.tanh(inner))


def gelu_slope(hidden):
    inner = gelu_coef * (hidden + 0.044715 * hidden * hidden * hidden)
    t = jnp.tanh(inner)
    return 0.5 * (1.0 + t) + 0.5 * hidden * (1.0 - t * t) * gelu_coef * (
        1.0 + 3.0 * 0.044715 * hidden * hidden
    )


def dot_nn(a, b):
    return lax.dot_general(a, b, (((1,), (0,)), ((), ())), preferred_element_type=F32)


def dot_nt(a, b):
    return lax.dot_general(a, b, (((1,), (1,)), ((), ())), preferred_element_type=F32)


def dot_tn(a, b):
    return lax.dot_general(a, b, (((0,), (0,)), ((), ())), preferred_element_type=F32)


def over(count, body, carry):
    for i in range(count):
        carry = body(i, carry)
    return carry


def lane_fold(v):
    total = v[:, 0:128]
    for i in range(1, v.shape[1] // 128):
        total = total + v[:, i * 128 : (i + 1) * 128]
    return total


def kernel(
    down, up, entry, labels, label_rows, evals,
    eval_out, logp_out, flog_out,
    w, x, g, rows, lab, wide, narrow, hid, act, scale,
    fb, r1, r2, s2, r3, s3, r4, dens, wd, merged, vin, picked,
    load_sem, ps, pr, cs, cr, as_, ar, bs, br, bfs, bfr, os_, orr, es, er, fs, fr,
    s1s, s1r, s2s, s2r, ys, yr, gas, gar, gbs, gbr, vs, vr,
):
    s = lax.axis_index("section")
    d = lax.axis_index("dp")
    h = s // 2
    c = s % 2
    yl = d // 16
    xx = (d // 4) % 4
    zz = d % 4
    y = 2 * h + yl
    u = xx * (1 - c) + zz * c
    v = zz * (1 - c) + xx * c

    def at(h_, c_, yl_, x_, z_):
        return {"section": h_ * 2 + c_, "dp": yl_ * 16 + x_ * 4 + z_}

    def at_uv(u_, v_):
        return at(h, c, yl, u_ * (1 - c) + v_ * c, v_ * (1 - c) + u_ * c)

    def at_y(y_, core=None):
        return at(y_ // 2, c if core is None else core, y_ % 2, xx, zz)

    partner = at(h, 1 - c, yl, xx, zz)
    swap = at(h, 1 - c, 1 - yl, xx, zz)
    across = at(1 - h, c, 1 - yl, xx, zz)
    after = at(1 - h, 1 - c, yl, xx, zz)
    third = at(1 - h, 1 - c, 1 - yl, xx, zz)
    a_peers = [None] + [at_uv((u + i) % 4, v) for i in range(1, 4)]
    b_peers = [None] + [at_uv(u, (v + i) % 4) for i in range(1, 4)]
    x_peers = [None] + [at(h, c, yl, (xx + i) % 4, zz) for i in range(1, 4)]
    z_peers = [None] + [at(h, c, yl, xx, (zz + i) % 4) for i in range(1, 4)]
    y_peers = [None] + [at_y((y + i) % 4) for i in range(1, 4)]

    def remote(src, dst, send, recv, to):
        return pltpu.make_async_remote_copy(
            src_ref=src, dst_ref=dst, send_sem=send, recv_sem=recv, device_id=to, device_id_type=MESH
        )

    barrier = pltpu.get_barrier_semaphore()
    everyone = [partner, swap, after, third] + a_peers[1:] + b_peers[1:] + y_peers[1:]
    for peer in everyone:
        pl.semaphore_signal(barrier, inc=1, device_id=peer, device_id_type=MESH)
    pl.semaphore_wait(barrier, len(everyone))

    far = 3 - y
    part = D // 16
    def cross(t, m):
        place = pl.ds((((u + 2 * t) % 4) * 4 + v) * part, part)
        return remote((down, up)[m].at[far, place], w.at[s, m, place], cs.at[t, m], cr.at[t, m], across)

    for t in range(2):
        for m in range(2):
            cross(t, m).start()
    beside = [
        remote(down.at[y], w.at[s, 0], ps.at[0], pr.at[0], partner),
        remote(up.at[y], w.at[s, 1], ps.at[1], pr.at[1], partner),
    ]
    moved = [
        remote(entry, x.at[0], es.at[0], er.at[0], swap),
        remote(labels.at[2 * h + 1 - yl], lab, es.at[1], er.at[1], swap),
    ]
    kept = [
        pltpu.make_async_copy(entry, x.at[0], load_sem.at[0]),
        pltpu.make_async_copy(labels.at[y], lab, load_sem.at[1]),
    ]

    @pl.when(c != yl)
    def _():
        for copy in moved:
            copy.start()

    @pl.when(c == yl)
    def _():
        for copy in kept:
            copy.start()

    for copy in beside:
        copy.start()
    loads = [
        pltpu.make_async_copy(down.at[y], w.at[s, 0], load_sem.at[2]),
        pltpu.make_async_copy(up.at[y], w.at[s, 1], load_sem.at[3]),
        pltpu.make_async_copy(label_rows, rows, load_sem.at[4]),
    ]
    for t in range(TASKS):
        for a in range(2):
            mine = pl.ds(pl.multiple_of((a * 16 + xx * 4 + zz) * 144, 16), 144)
            for m, whole in enumerate((down, up)):
                sem = load_sem.at[16 + 4 * t + 2 * a + m]
                loads.append(pltpu.make_async_copy(whole.at[t, mine], wd.at[t, m, a], sem))
    for copy in loads:
        copy.start()
    eval_load = pltpu.make_async_copy(evals, vin, load_sem.at[13])

    @pl.when(s == 0)
    def _():
        eval_load.start()

    lr = 2 * (1 - h) + c

    def piece(m, o, e):
        return w.at[lr, m, pl.ds((((u + o) % 4) * 4 + (v + e) % 4) * part, part)]

    def along_a(m, i):
        return remote(piece(m, 0, 0), piece(m, 0, 0), as_.at[m, i], ar.at[m, i], a_peers[i])

    def along_b(m, o, j):
        return remote(piece(m, o, 0), piece(m, o, 0), bs.at[m, o, j], br.at[m, o, j], b_peers[j])

    def further(m, o):
        view = piece(m, o, 3 if m == 0 else 1)
        return remote(view, view, bfs.at[m, o], bfr.at[m, o], b_peers[1 if m == 0 else 3])

    def to_b(o, m):
        along_b(m, o, 1).start()
        along_b(m, o, 3).start()

    def to_further(o):
        along_b(0, o, 1).wait_recv()
        further(0, o).start()
        along_b(1, o, 3).wait_recv()
        further(1, o).start()

    for m in range(2):
        cross(0, m).wait_recv()
        along_a(m, 1).start()
        along_a(m, 3).start()
        to_b(0, m)
    for m in range(2):
        for o in (1, 3):
            along_a(m, 4 - o).wait_recv()
            to_b(o, m)
    to_further(0)
    for m in range(2):
        cross(1, m).wait_recv()
        to_b(2, m)
    o_sends = []
    for o in (1, 3, 2):
        to_further(o)
    for o in (0, 1, 3, 2):
        along_b(0, o, 3).wait_recv()
        along_b(1, o, 1).wait_recv()
        for m in range(2):
            further(m, o).wait_recv()
        view = w.at[lr, :, pl.ds(((u + o) % 4) * BLK, BLK)]
        copy = remote(view, view, os_.at[o], orr.at[o], partner)
        copy.start()
        o_sends.append(copy)

    @pl.when(c != yl)
    def _():
        for copy in moved:
            copy.wait()

    @pl.when(c == yl)
    def _():
        for copy in kept:
            copy.wait()

    for copy in beside:
        copy.wait()
    for copy in loads:
        copy.wait()
    for m in range(2):
        for t in range(2):
            cross(t, m).wait_send()
        for j in (1, 3):
            along_a(m, j).wait_send()
            for o in range(4):
                along_b(m, o, j).wait_send()
        for o in range(4):
            further(m, o).wait_send()
    for copy in o_sends:
        copy.wait()

    zero = jnp.zeros((N, 128), F32)

    def cols(f, size=TILE):
        return pl.ds(f * size, size)

    def first(f, carry):
        total, acc = carry
        xt = x[0, :, cols(f)]
        xf = xt.astype(F32)
        return total + lane_fold(xf * xf), acc + dot_nn(xt, w[0, 0, cols(f), :])

    total, acc = over(D // TILE, first, (zero, zero))
    for k in range(4):
        sk = lax.rsqrt(jnp.sum(total, axis=1, keepdims=True) * (1.0 / D) + norm_eps)
        hk = sk * acc
        scale[k] = jnp.broadcast_to(sk, (N, 128))
        hid[k] = hk
        ak = gelu_value(hk).astype(BF16)
        act[k] = ak

        def step(f, carry, k=k, ak=ak):
            total, acc = carry
            new = (x[k, :, cols(f)].astype(F32) + dot_nt(ak, w[k, 1, cols(f), :])).astype(BF16)
            x[k + 1, :, cols(f)] = new
            nf = new.astype(F32)
            if k < 3:
                more = dot_nn(new, w[k + 1, 0, cols(f), :])
            else:
                more = dot_nt(new, rows[:, cols(f)])
            return total + lane_fold(nf * nf), acc + more

        width = R if k < 3 else LABELS
        total, acc = over(D // TILE, step, (zero, jnp.zeros((N, width), F32)))

    sy = lax.rsqrt(jnp.sum(total, axis=1, keepdims=True) * (1.0 / D) + norm_eps)
    logits = sy * acc
    bent = jnp.tanh(logits * (1.0 / soft_cap))
    capped = soft_cap * bent
    logp = capped - jnp.log(jnp.sum(jnp.exp(capped), axis=1, keepdims=True))
    word = lax.broadcasted_iota(jnp.int32, (LABELS, ROWS), 0)
    marks = [jnp.where(word == lab[m : m + 1, :], 1.0, 0.0) for m in range(MICRO)]
    hot = jnp.concatenate([jnp.transpose(mark) for mark in marks], axis=0)
    for m in range(MICRO):
        part_logp = jnp.transpose(logp[m * ROWS : (m + 1) * ROWS, :])
        picked[m : m + 1, :] = jnp.sum(part_logp * marks[m], axis=0, keepdims=True)
    give = remote(picked, logp_out, es.at[2], er.at[2], swap)
    hold = pltpu.make_async_copy(picked, logp_out, load_sem.at[14])

    @pl.when(c != yl)
    def _():
        give.start()

    @pl.when(c == yl)
    def _():
        hold.start()

    e = ((jnp.exp(logp) - hot) * (1.0 - bent * bent)).astype(BF16)
    mean = jnp.sum(e.astype(F32) * logits, axis=1, keepdims=True) * (1.0 / D)
    sm = sy * mean

    def squares(k, f, gy):
        nf = x[k, :, cols(f)].astype(F32) * scale[k][:, 0:1]
        gf = gy.astype(F32)
        wide[0, :, cols(f)] = (nf * nf).astype(BF16)
        wide[1, :, cols(f)] = (gf * gf).astype(BF16)

    def head(f, acc):
        back = dot_nn(e, rows[:, cols(f)])
        gy = (sy * (back - x[4, :, cols(f)].astype(F32) * sm)).astype(BF16)
        g[:, cols(f)] = gy
        squares(3, f, gy)
        return acc + dot_nn(gy, w[3, 1, cols(f), :])

    ga = over(D // TILE, head, zero)

    def give_half(k):
        return remote(fb.at[k, 1 - c], r1.at[k], fs.at[k], fr.at[k], partner)

    def stage_one(k, i, view):
        return remote(view, r2.at[k, i - 1], s1s.at[k, i], s1r.at[k, i], a_peers[i])

    def open_sum(k):
        remote(fb.at[k, c], r1.at[k], fs.at[k], fr.at[k], partner).wait_recv()
        for a in range(2):
            for b in range(4):
                fb[k, c, a, b] = (fb[k, c, a, b].astype(F32) + r1[k, a, b].astype(F32)).astype(BF16)

        @pl.when(c == 0)
        def _():
            for i in (2, 1, 3):
                stage_one(k, i, fb.at[k, 0, :, (u + i) % 4]).start()

        @pl.when(c == 1)
        def _():
            for i in (2, 1, 3):
                stage_one(k, i, fb.at[k, 1, :, :, (u + i) % 4]).start()

    def stage_two(k, i):
        return remote(s2.at[k, :, (v + i) % 4], r3.at[k, i - 1], s2s.at[k, i], s2r.at[k, i], b_peers[i])

    def middle_sum(k):
        for i in range(1, 4):
            stage_one(k, i, r2.at[k, i - 1]).wait_recv()

        def add_with(load):
            for a in range(2):
                for b in range(4):
                    value = load(a, b).astype(F32)
                    for i in range(3):
                        value = value + r2[k, i, a, b].astype(F32)
                    s2[k, a, b] = value.astype(BF16)

        @pl.when(c == 0)
        def _():
            add_with(lambda a, b: fb[k, 0, a, u, b])

        @pl.when(c == 1)
        def _():
            add_with(lambda a, b: fb[k, 1, a, b, u])

        for i in (2, 1, 3):
            stage_two(k, i).start()

    def along_y(k, q):
        y_ = 2 * (k // 2) + q
        slot = (y_ + 4 - y) % 4
        return remote(s3.at[k], r4.at[slot, c], ys.at[k, q], yr.at[slot, c], at(k // 2, k % 2, q, xx, zz))

    def is_me(k, q):
        return (h == k // 2) & (c == k % 2) & (yl == q)

    def last_sum(k):
        for i in range(1, 4):
            stage_two(k, i).wait_recv()
        for a in range(2):
            value = s2[k, a, v].astype(F32)
            for i in range(3):
                value = value + r3[k, i, a].astype(F32)
            s3[k, a] = value.astype(BF16)
        for q in range(2):

            @pl.when(jnp.logical_not(is_me(k, q)))
            def _(q=q):
                along_y(k, q).start()

            @pl.when(is_me(k, q))
            def _():
                r4[0, c] = s3[k]

    def block(m, x_, z_):
        return merged.at[m, :, x_, z_]

    def gather_a(m, i):
        peers = (x_peers, z_peers)[m]
        return remote(block(m, xx, zz), block(m, xx, zz), gas.at[m, i], gar.at[m, i], peers[i])

    def gathered(m, i, e):
        x_ = (xx + 4 - i) % 4 if m == 0 else (xx + e) % 4
        z_ = (zz + 4 - i) % 4 if m == 1 else (zz + e) % 4
        return x_, z_

    def gather_b(m, i, j):
        view = block(m, *gathered(m, i, 0))
        return remote(view, view, gbs.at[m, i, j], gbr.at[m, i, j], (z_peers, x_peers)[m][j])

    def gather_on(m, i, a):
        view = merged.at[(m, a, *gathered(m, i, 3 if a == 0 else 1))]
        to = (z_peers, x_peers)[m][1 if a == 0 else 3]
        return remote(view, view, gbs.at[m, i, 2 * a], gbr.at[m, i, 2 * a], to)

    def merge():
        for i in range(4):
            for m in range(2):
                arrived = remote(r4.at[i, m], r4.at[i, m], ys.at[0, 0], yr.at[i, m], partner)
                if i:
                    arrived.wait_recv()
                else:

                    @pl.when(c != m)
                    def _(arrived=arrived):
                        arrived.wait_recv()

        for m in range(2):
            for a in range(2):
                den = jnp.zeros((144, 128), F32)
                num = jnp.zeros((144, 128), F32)
                for i in range(4):
                    t = (y + 4 - i) % 4
                    value = r4[i, m, a].astype(F32)
                    den = den + value
                    num = num + value * wd[t, m, a].astype(F32)
                den = den + merge_eps
                dens[a, m] = den
                merged[m, a, xx, zz] = (num / den).astype(BF16)
            for i in (1, 3, 2):
                gather_a(m, i).start()

    def pass_on():
        def onward(m, i):
            gather_b(m, i, 1).wait_recv()
            gather_on(m, i, 0).start()
            gather_b(m, i, 3).wait_recv()
            gather_on(m, i, 1).start()

        def direct(m, i):
            if i:
                gather_a(m, i).wait_recv()
            gather_b(m, i, 1).start()
            gather_b(m, i, 3).start()

        for i in (0, 1, 3):
            for m in range(2):
                direct(m, i)
        for m in range(2):
            onward(m, 0)
        for m in range(2):
            direct(m, 2)
        for i in (1, 3, 2):
            for m in range(2):
                onward(m, i)

    for k in (3, 2, 1, 0):
        hk = hid[k]
        sk = scale[k][:, 0:1]
        gh = (ga * gelu_slope(hk)).astype(BF16)
        ghf = gh.astype(F32)
        mean = jnp.sum(ghf * hk, axis=1, keepdims=True) * (1.0 / D)
        narrow[0] = (ghf * ghf).astype(BF16)
        af = act[k].astype(F32)
        narrow[1] = (af * af).astype(BF16)

        for m in (1 - c, c):
            thin = narrow[m]
            for b in range(4):
                value = dot_tn(wide[m, :, cols(b, BLK)], thin).astype(BF16)
                fb[k, m, b // 2, pl.ds((b % 2) * 2, 2)] = value.reshape(2, 4, 144, 128)
            if m is not c:
                give_half(k).start()
        if k == 0:
            break

        def step(f, acc, k=k, gh=gh, sk=sk, sm=sk * mean):
            back = dot_nt(gh, w[k, 0, cols(f), :])
            gy = (
                g[:, cols(f)].astype(F32) + (sk * back - x[k, :, cols(f)].astype(F32) * (sk * sm))
            ).astype(BF16)
            g[:, cols(f)] = gy
            squares(k - 1, f, gy)
            return acc + dot_nn(gy, w[k - 1, 1, cols(f), :])

        ga = over(D // TILE, step, zero)
        open_sum(k)

    middle_sum(3)
    open_sum(0)
    last_sum(3)
    middle_sum(2)
    last_sum(2)
    middle_sum(1)
    last_sum(1)
    middle_sum(0)

    @pl.when(s != 0)
    def _():
        merge()

    last_sum(0)

    @pl.when(s == 0)
    def _():
        merge()

    pass_on()

    def hand_on(b, to):
        return remote(eval_out.at[:, cols(b, BLK)], vin.at[:, cols(b, BLK)], vs.at[b], vr.at[b], to)

    @pl.when(s == 0)
    def _():
        eval_load.wait()

    def weights(m, b):
        return merged[m, b // 2, pl.ds((b % 2) * 2, 2)].reshape(BLK, 128)

    for i in range(4):
        for a in range(2):
            gather_on(0, i, a).wait_recv()
    total = jnp.zeros((ROWS, 128), F32)
    acc = jnp.zeros((ROWS, 128), F32)
    for b in range(4):

        @pl.when(s != 0)
        def _(b=b):
            hand_on(b, partner).wait_recv()

        vt = vin[:, cols(b, BLK)]
        vf = vt.astype(F32)
        total = total + lane_fold(vf * vf)
        acc = acc + dot_nn(vt, weights(0, b))
    sv = lax.rsqrt(jnp.sum(total, axis=1, keepdims=True) * (1.0 / D) + norm_eps)
    av = gelu_value(sv * acc).astype(BF16)
    for i in range(4):
        for a in range(2):
            gather_on(1, i, a).wait_recv()
    for b in range(4):
        eval_out[:, cols(b, BLK)] = (
            vin[:, cols(b, BLK)].astype(F32) + dot_nt(av, weights(1, b))
        ).astype(BF16)

        @pl.when(c == 0)
        def _(b=b):
            hand_on(b, partner).start()

        @pl.when(s == 1)
        def _(b=b):
            hand_on(b, after).start()

    for m in range(2):
        flog_out[m] = jnp.log(dens[yl, m])
    for b in range(4):

        @pl.when(s != 3)
        def _(b=b):
            hand_on(b, partner).wait_send()

    for m in range(2):
        for j in range(1, 4):
            gather_a(m, j).wait_send()
        for i in range(4):
            for j in (1, 3):
                gather_b(m, i, j).wait_send()
            for a in range(2):
                gather_on(m, i, a).wait_send()
    for k in range(4):
        for q in range(2):

            @pl.when(jnp.logical_not(is_me(k, q)))
            def _(k=k, q=q):
                along_y(k, q).wait_send()

        give_half(k).wait_send()
        for i in range(1, 4):
            stage_one(k, i, r2.at[k, i - 1]).wait_send()
            stage_two(k, i).wait_send()

    @pl.when(c != yl)
    def _():
        give.wait()

    @pl.when(c == yl)
    def _():
        hold.wait()


def local(entry_states, down_proj, up_proj, label_rows, sampled_labels, eval_states):
    vmem = pl.BlockSpec(memory_space=pltpu.VMEM)
    hbm = pl.BlockSpec(memory_space=pl.ANY)
    dma = pltpu.SemaphoreType.DMA
    eval_out, logp, flog = pl.pallas_call(
        kernel,
        out_shape=(
            jax.ShapeDtypeStruct((ROWS, D), BF16),
            jax.ShapeDtypeStruct((MICRO, ROWS), F32),
            jax.ShapeDtypeStruct((2, 144, 128), F32),
        ),
        in_specs=[hbm] * 6,
        out_specs=(vmem, vmem, vmem),
        scratch_shapes=[
            pltpu.VMEM((4, 2, D, R), BF16),
            pltpu.VMEM((5, N, D), BF16),
            pltpu.VMEM((N, D), BF16),
            pltpu.VMEM((LABELS, D), BF16),
            pltpu.VMEM((MICRO, ROWS), jnp.int32),
            pltpu.VMEM((2, N, D), BF16),
            pltpu.VMEM((2, N, R), BF16),
            pltpu.VMEM((4, N, R), F32),
            pltpu.VMEM((4, N, R), BF16),
            pltpu.VMEM((4, N, 128), F32),
            pltpu.VMEM((4, 2, 2, 4, 4, 144, 128), BF16),
            pltpu.VMEM((4, 2, 4, 4, 144, 128), BF16),
            pltpu.VMEM((4, 3, 2, 4, 144, 128), BF16),
            pltpu.VMEM((4, 2, 4, 144, 128), BF16),
            pltpu.VMEM((4, 3, 2, 144, 128), BF16),
            pltpu.VMEM((4, 2, 144, 128), BF16),
            pltpu.VMEM((4, 2, 2, 144, 128), BF16),
            pltpu.VMEM((2, 2, 144, 128), F32),
            pltpu.VMEM((4, 2, 2, 144, 128), BF16),
            pltpu.VMEM((2, 2, 4, 4, 144, 128), BF16),
            pltpu.VMEM((ROWS, D), BF16),
            pltpu.VMEM((MICRO, ROWS), F32),
            dma((32,)),
            dma((2,)), dma((2,)),
            dma((2, 2)), dma((2, 2)),
            dma((2, 4)), dma((2, 4)),
            dma((2, 4, 4)), dma((2, 4, 4)),
            dma((2, 4)), dma((2, 4)),
            dma((4,)), dma((4,)),
            dma((3,)), dma((3,)),
            dma((4,)), dma((4,)),
            dma((4, 4)), dma((4, 4)),
            dma((4, 4)), dma((4, 4)),
            dma((4, 2)), dma((4, 2)),
            dma((2, 4)), dma((2, 4)),
            dma((2, 4, 4)), dma((2, 4, 4)),
            dma((4,)), dma((4,)),
        ],
        compiler_params=pltpu.CompilerParams(
            collective_id=0, has_side_effects=True, vmem_limit_bytes=67043328
        ),
        name="merge",
    )(
        down_proj.reshape(TASKS, D, R),
        up_proj.reshape(TASKS, D, R),
        entry_states.reshape(N, D),
        sampled_labels,
        label_rows,
        eval_states,
    )
    return (
        eval_out[None],
        logp[None],
        flog[None],
    )


def solution(mesh):
    placed = (
        P(None, "dp", None),
        P("section", None, None, None),
        P("section", None, None, None),
        P(),
        P(None, None, "dp"),
        P("dp", None),
    )
    return jax.shard_map(
        local,
        mesh=mesh,
        in_specs=placed,
        out_specs=(
            P("section", "dp", None),
            P("section", None, "dp"),
            P("section", None, "dp", None),
        ),
        check_vma=False,
    )
```

```python
import jax
import jax.numpy as jnp
from jax import lax
from jax.experimental import pallas as pl
from jax.experimental.pallas import tpu as pltpu
from jax.sharding import PartitionSpec as P

norm_eps = 1e-06
merge_eps = 1e-06
soft_cap = 30.0
gelu_coef = 0.7978845608028654

D = 4608
R = 128
LABELS = 256
TASKS = 4
MICRO = 5
ROWS = 32
N = MICRO * ROWS
TILE = 512
BLK = D // 4
F32 = jnp.float32
BF16 = jnp.bfloat16
MESH = pl.DeviceIdType.MESH


def gelu_value(hidden):
    inner = gelu_coef * (hidden + 0.044715 * hidden * hidden * hidden)
    return 0.5 * hidden * (1.0 + jnp.tanh(inner))


def gelu_slope(hidden):
    inner = gelu_coef * (hidden + 0.044715 * hidden * hidden * hidden)
    t = jnp.tanh(inner)
    return 0.5 * (1.0 + t) + 0.5 * hidden * (1.0 - t * t) * gelu_coef * (
        1.0 + 3.0 * 0.044715 * hidden * hidden
    )


def dot_nn(a, b):
    return lax.dot_general(a, b, (((1,), (0,)), ((), ())), preferred_element_type=F32)


def dot_nt(a, b):
    return lax.dot_general(a, b, (((1,), (1,)), ((), ())), preferred_element_type=F32)


def dot_tn(a, b):
    return lax.dot_general(a, b, (((0,), (0,)), ((), ())), preferred_element_type=F32)


def over(count, body, carry):
    for i in range(count):
        carry = body(i, carry)
    return carry


def lane_fold(v):
    total = v[:, 0:128]
    for i in range(1, v.shape[1] // 128):
        total = total + v[:, i * 128 : (i + 1) * 128]
    return total


def kernel(
    down, up, entry, labels, label_rows, evals,
    eval_out, logp_out, flog_out,
    w, x, g, rows, lab, wide, narrow, hid, act, scale,
    fb, r1, r2, s2, r3, s3, r4, dens, wd, merged, vin, picked,
    load_sem, ps, pr, cs, cr, as_, ar, bs, br, bfs, bfr, os_, orr, es, er, fs, fr,
    s1s, s1r, s2s, s2r, ys, yr, gas, gar, gbs, gbr, vs, vr,
):
    s = lax.axis_index("section")
    d = lax.axis_index("dp")
    h = s // 2
    c = s % 2
    yl = d // 16
    xx = (d // 4) % 4
    zz = d % 4
    y = 2 * h + yl
    u = xx * (1 - c) + zz * c
    v = zz * (1 - c) + xx * c

    def at(h_, c_, yl_, x_, z_):
        return {"section": h_ * 2 + c_, "dp": yl_ * 16 + x_ * 4 + z_}

    def at_uv(u_, v_):
        return at(h, c, yl, u_ * (1 - c) + v_ * c, v_ * (1 - c) + u_ * c)

    def at_y(y_, core=None):
        return at(y_ // 2, c if core is None else core, y_ % 2, xx, zz)

    partner = at(h, 1 - c, yl, xx, zz)
    swap = at(h, 1 - c, 1 - yl, xx, zz)
    across = at(1 - h, c, 1 - yl, xx, zz)
    after = at(1 - h, 1 - c, yl, xx, zz)
    third = at(1 - h, 1 - c, 1 - yl, xx, zz)
    a_peers = [None] + [at_uv((u + i) % 4, v) for i in range(1, 4)]
    b_peers = [None] + [at_uv(u, (v + i) % 4) for i in range(1, 4)]
    x_peers = [None] + [at(h, c, yl, (xx + i) % 4, zz) for i in range(1, 4)]
    z_peers = [None] + [at(h, c, yl, xx, (zz + i) % 4) for i in range(1, 4)]
    y_peers = [None] + [at_y((y + i) % 4) for i in range(1, 4)]

    def remote(src, dst, send, recv, to):
        return pltpu.make_async_remote_copy(
            src_ref=src, dst_ref=dst, send_sem=send, recv_sem=recv, device_id=to, device_id_type=MESH
        )

    barrier = pltpu.get_barrier_semaphore()
    everyone = [partner, swap, after, third] + a_peers[1:] + b_peers[1:] + y_peers[1:]
    for peer in everyone:
        pl.semaphore_signal(barrier, inc=1, device_id=peer, device_id_type=MESH)
    pl.semaphore_wait(barrier, len(everyone))

    far = 3 - y
    part = D // 16
    def cross(t, m):
        place = pl.ds((((u + 2 * t) % 4) * 4 + v) * part, part)
        return remote((down, up)[m].at[far, place], w.at[s, m, place], cs.at[t, m], cr.at[t, m], across)

    for m in range(2):
        cross(0, m).start()
    beside = [
        remote(down.at[y], w.at[s, 0], ps.at[0], pr.at[0], partner),
        remote(up.at[y], w.at[s, 1], ps.at[1], pr.at[1], partner),
    ]
    moved = [
        remote(entry, x.at[0], es.at[0], er.at[0], swap),
        remote(labels.at[2 * h + 1 - yl], lab, es.at[1], er.at[1], swap),
    ]
    kept = [
        pltpu.make_async_copy(entry, x.at[0], load_sem.at[0]),
        pltpu.make_async_copy(labels.at[y], lab, load_sem.at[1]),
    ]

    @pl.when(c != yl)
    def _():
        for copy in moved:
            copy.start()

    @pl.when(c == yl)
    def _():
        for copy in kept:
            copy.start()

    for copy in beside:
        copy.start()
    loads = [
        pltpu.make_async_copy(down.at[y], w.at[s, 0], load_sem.at[2]),
        pltpu.make_async_copy(up.at[y], w.at[s, 1], load_sem.at[3]),
        pltpu.make_async_copy(label_rows, rows, load_sem.at[4]),
    ]
    for t in range(TASKS):
        for a in range(2):
            mine = pl.ds(pl.multiple_of((a * 16 + xx * 4 + zz) * 144, 16), 144)
            for m, whole in enumerate((down, up)):
                sem = load_sem.at[16 + 4 * t + 2 * a + m]
                loads.append(pltpu.make_async_copy(whole.at[t, mine], wd.at[t, m, a], sem))
    for copy in loads:
        copy.start()
    eval_load = pltpu.make_async_copy(evals, vin, load_sem.at[13])

    @pl.when(s == 0)
    def _():
        eval_load.start()

    lr = 2 * (1 - h) + c

    def piece(m, o, e):
        return w.at[lr, m, pl.ds((((u + o) % 4) * 4 + (v + e) % 4) * part, part)]

    def along_a(m, i):
        return remote(piece(m, 0, 0), piece(m, 0, 0), as_.at[m, i], ar.at[m, i], a_peers[i])

    def along_b(m, o, j):
        return remote(piece(m, o, 0), piece(m, o, 0), bs.at[m, o, j], br.at[m, o, j], b_peers[j])

    def further(m, o):
        view = piece(m, o, 3 if m == 0 else 1)
        return remote(view, view, bfs.at[m, o], bfr.at[m, o], b_peers[1 if m == 0 else 3])

    def to_b(o, m):
        along_b(m, o, 1).start()
        along_b(m, o, 3).start()

    def to_further(o):
        along_b(0, o, 1).wait_recv()
        further(0, o).start()
        along_b(1, o, 3).wait_recv()
        further(1, o).start()

    for m in range(2):
        cross(0, m).wait_recv()
        cross(1, m).start()
        along_a(m, 1).start()
        along_a(m, 3).start()
        to_b(0, m)
    for m in range(2):
        for o in (1, 3):
            along_a(m, 4 - o).wait_recv()
            to_b(o, m)
    to_further(0)
    for m in range(2):
        cross(1, m).wait_recv()
        to_b(2, m)
    o_sends = []
    for o in (1, 3, 2):
        to_further(o)
    for o in (0, 1, 3, 2):
        along_b(0, o, 3).wait_recv()
        along_b(1, o, 1).wait_recv()
        for m in range(2):
            further(m, o).wait_recv()
        view = w.at[lr, :, pl.ds(((u + o) % 4) * BLK, BLK)]
        copy = remote(view, view, os_.at[o], orr.at[o], partner)
        copy.start()
        o_sends.append(copy)

    @pl.when(c != yl)
    def _():
        for copy in moved:
            copy.wait()

    @pl.when(c == yl)
    def _():
        for copy in kept:
            copy.wait()

    for copy in beside:
        copy.wait()
    for copy in loads:
        copy.wait()
    for m in range(2):
        for t in range(2):
            cross(t, m).wait_send()
        for j in (1, 3):
            along_a(m, j).wait_send()
            for o in range(4):
                along_b(m, o, j).wait_send()
        for o in range(4):
            further(m, o).wait_send()
    for copy in o_sends:
        copy.wait()

    zero = jnp.zeros((N, 128), F32)

    def cols(f, size=TILE):
        return pl.ds(f * size, size)

    def first(f, carry):
        total, acc = carry
        xt = x[0, :, cols(f)]
        xf = xt.astype(F32)
        return total + lane_fold(xf * xf), acc + dot_nn(xt, w[0, 0, cols(f), :])

    total, acc = over(D // TILE, first, (zero, zero))
    for k in range(4):
        sk = lax.rsqrt(jnp.sum(total, axis=1, keepdims=True) * (1.0 / D) + norm_eps)
        hk = sk * acc
        scale[k] = jnp.broadcast_to(sk, (N, 128))
        hid[k] = hk
        ak = gelu_value(hk).astype(BF16)
        act[k] = ak

        def step(f, carry, k=k, ak=ak):
            total, acc = carry
            new = (x[k, :, cols(f)].astype(F32) + dot_nt(ak, w[k, 1, cols(f), :])).astype(BF16)
            x[k + 1, :, cols(f)] = new
            nf = new.astype(F32)
            if k < 3:
                more = dot_nn(new, w[k + 1, 0, cols(f), :])
            else:
                more = dot_nt(new, rows[:, cols(f)])
            return total + lane_fold(nf * nf), acc + more

        width = R if k < 3 else LABELS
        total, acc = over(D // TILE, step, (zero, jnp.zeros((N, width), F32)))

    sy = lax.rsqrt(jnp.sum(total, axis=1, keepdims=True) * (1.0 / D) + norm_eps)
    logits = sy * acc
    bent = jnp.tanh(logits * (1.0 / soft_cap))
    capped = soft_cap * bent
    logp = capped - jnp.log(jnp.sum(jnp.exp(capped), axis=1, keepdims=True))
    word = lax.broadcasted_iota(jnp.int32, (LABELS, ROWS), 0)
    marks = [jnp.where(word == lab[m : m + 1, :], 1.0, 0.0) for m in range(MICRO)]
    hot = jnp.concatenate([jnp.transpose(mark) for mark in marks], axis=0)
    for m in range(MICRO):
        part_logp = jnp.transpose(logp[m * ROWS : (m + 1) * ROWS, :])
        picked[m : m + 1, :] = jnp.sum(part_logp * marks[m], axis=0, keepdims=True)
    give = remote(picked, logp_out, es.at[2], er.at[2], swap)
    hold = pltpu.make_async_copy(picked, logp_out, load_sem.at[14])

    @pl.when(c != yl)
    def _():
        give.start()

    @pl.when(c == yl)
    def _():
        hold.start()

    e = ((jnp.exp(logp) - hot) * (1.0 - bent * bent)).astype(BF16)
    mean = jnp.sum(e.astype(F32) * logits, axis=1, keepdims=True) * (1.0 / D)
    sm = sy * mean

    def squares(k, f, gy):
        nf = x[k, :, cols(f)].astype(F32) * scale[k][:, 0:1]
        gf = gy.astype(F32)
        wide[0, :, cols(f)] = (nf * nf).astype(BF16)
        wide[1, :, cols(f)] = (gf * gf).astype(BF16)

    def head(f, acc):
        back = dot_nn(e, rows[:, cols(f)])
        gy = (sy * (back - x[4, :, cols(f)].astype(F32) * sm)).astype(BF16)
        g[:, cols(f)] = gy
        squares(3, f, gy)
        return acc + dot_nn(gy, w[3, 1, cols(f), :])

    ga = over(D // TILE, head, zero)

    def give_half(k):
        return remote(fb.at[k, 1 - c], r1.at[k], fs.at[k], fr.at[k], partner)

    up_one, down_one = (u + 1) % 4, (u + 3) % 4

    def stage_one(k, i, view):
        return remote(view, r2.at[k, i], s1s.at[k, i], s1r.at[k, i], a_peers[1 if i in (0, 1, 4) else 3])

    def with_block(k, body):
        @pl.when(c == 0)
        def _():
            body(lambda t, a: fb.at[k, 0, a, t])

        @pl.when(c == 1)
        def _():
            body(lambda t, a: fb.at[k, 1, a, :, t])

    def open_sum(k):
        remote(fb.at[k, c], r1.at[k], fs.at[k], fr.at[k], partner).wait_recv()
        for a in range(2):
            for b in range(4):
                fb[k, c, a, b] = (fb[k, c, a, b].astype(F32) + r1[k, a, b].astype(F32)).astype(BF16)

        def send(view):
            stage_one(k, 4, view((u + 2) % 4, 0)).start()
            stage_one(k, 5, view((u + 2) % 4, 1)).start()

        with_block(k, send)

    def direct_sum(k):
        def send(view):
            stage_one(k, 1, view(up_one, 1)).start()
            stage_one(k, 3, view(down_one, 0)).start()

        with_block(k, send)

    def relay_sum(k):
        for i in (4, 5):
            stage_one(k, i, r2.at[k, i]).wait_recv()

        def send(view):
            for i, t, a in ((4, up_one, 0), (5, down_one, 1)):
                own_part = view(t, a)
                for b in range(4):
                    r2[k, i, b] = (r2[k, i, b].astype(F32) + own_part[b].astype(F32)).astype(BF16)
                stage_one(k, 0 if i == 4 else 2, r2.at[k, i]).start()

        with_block(k, send)

    def stage_two(k, i):
        return remote(s2.at[k, :, (v + i) % 4], r3.at[k, i - 1], s2s.at[k, i], s2r.at[k, i], b_peers[i])

    def middle_sum(k):
        for i in range(4):
            stage_one(k, i, r2.at[k, i]).wait_recv()

        def add(view):
            for a, pair in ((0, (0, 3)), (1, (1, 2))):
                own_part = view(u, a)
                for b in range(4):
                    value = own_part[b].astype(F32)
                    for i in pair:
                        value = value + r2[k, i, b].astype(F32)
                    s2[k, a, b] = value.astype(BF16)

        with_block(k, add)
        for i in (2, 1, 3):
            stage_two(k, i).start()

    def along_y(k, q):
        y_ = 2 * (k // 2) + q
        slot = (y_ + 4 - y) % 4
        return remote(s3.at[k], r4.at[slot, c], ys.at[k, q], yr.at[slot, c], at(k // 2, k % 2, q, xx, zz))

    def is_me(k, q):
        return (h == k // 2) & (c == k % 2) & (yl == q)

    def last_sum(k):
        for i in range(1, 4):
            stage_two(k, i).wait_recv()
        for a in range(2):
            value = s2[k, a, v].astype(F32)
            for i in range(3):
                value = value + r3[k, i, a].astype(F32)
            s3[k, a] = value.astype(BF16)
        for q in range(2):

            @pl.when(jnp.logical_not(is_me(k, q)))
            def _(q=q):
                along_y(k, q).start()

            @pl.when(is_me(k, q))
            def _():
                r4[0, c] = s3[k]

    def block(m, x_, z_):
        return merged.at[m, :, x_, z_]

    def gather_a(m, i):
        peers = (x_peers, z_peers)[m]
        return remote(block(m, xx, zz), block(m, xx, zz), gas.at[m, i], gar.at[m, i], peers[i])

    def gathered(m, i, e):
        x_ = (xx + 4 - i) % 4 if m == 0 else (xx + e) % 4
        z_ = (zz + 4 - i) % 4 if m == 1 else (zz + e) % 4
        return x_, z_

    def gather_b(m, i, j):
        view = block(m, *gathered(m, i, 0))
        return remote(view, view, gbs.at[m, i, j], gbr.at[m, i, j], (z_peers, x_peers)[m][j])

    def gather_on(m, i, a):
        view = merged.at[(m, a, *gathered(m, i, 3 if a == 0 else 1))]
        to = (z_peers, x_peers)[m][1 if a == 0 else 3]
        return remote(view, view, gbs.at[m, i, 2 * a], gbr.at[m, i, 2 * a], to)

    def merge():
        for i in range(4):
            for m in range(2):
                arrived = remote(r4.at[i, m], r4.at[i, m], ys.at[0, 0], yr.at[i, m], partner)
                if i:
                    arrived.wait_recv()
                else:

                    @pl.when(c != m)
                    def _(arrived=arrived):
                        arrived.wait_recv()

        for m in range(2):
            for a in range(2):
                den = jnp.zeros((144, 128), F32)
                num = jnp.zeros((144, 128), F32)
                for i in range(4):
                    t = (y + 4 - i) % 4
                    value = r4[i, m, a].astype(F32)
                    den = den + value
                    num = num + value * wd[t, m, a].astype(F32)
                den = den + merge_eps
                dens[a, m] = den
                merged[m, a, xx, zz] = (num / den).astype(BF16)
            for i in (1, 3, 2):
                gather_a(m, i).start()

    def pass_on():
        def onward(m, i):
            gather_b(m, i, 1).wait_recv()
            gather_on(m, i, 0).start()
            gather_b(m, i, 3).wait_recv()
            gather_on(m, i, 1).start()

        def direct(m, i):
            if i:
                gather_a(m, i).wait_recv()
            gather_b(m, i, 1).start()
            gather_b(m, i, 3).start()

        for i in (0, 1, 3):
            for m in range(2):
                direct(m, i)
        for m in range(2):
            onward(m, 0)
        for m in range(2):
            direct(m, 2)
        for i in (1, 3, 2):
            for m in range(2):
                onward(m, i)

    for k in (3, 2, 1, 0):
        hk = hid[k]
        sk = scale[k][:, 0:1]
        gh = (ga * gelu_slope(hk)).astype(BF16)
        ghf = gh.astype(F32)
        mean = jnp.sum(ghf * hk, axis=1, keepdims=True) * (1.0 / D)
        narrow[0] = (ghf * ghf).astype(BF16)
        af = act[k].astype(F32)
        narrow[1] = (af * af).astype(BF16)

        for m in (1 - c, c):
            thin = narrow[m]
            for b in range(4):
                value = dot_tn(wide[m, :, cols(b, BLK)], thin).astype(BF16)
                fb[k, m, b // 2, pl.ds((b % 2) * 2, 2)] = value.reshape(2, 4, 144, 128)
            if m is not c:
                give_half(k).start()
        if k == 0:
            break

        def step(f, acc, k=k, gh=gh, sk=sk, sm=sk * mean):
            back = dot_nt(gh, w[k, 0, cols(f), :])
            gy = (
                g[:, cols(f)].astype(F32) + (sk * back - x[k, :, cols(f)].astype(F32) * (sk * sm))
            ).astype(BF16)
            g[:, cols(f)] = gy
            squares(k - 1, f, gy)
            return acc + dot_nn(gy, w[k - 1, 1, cols(f), :])

        ga = over(D // TILE, step, zero)
        if k == 3:
            open_sum(3)
            direct_sum(3)
        if k == 2:
            relay_sum(3)
            open_sum(2)
            direct_sum(2)
        if k == 1:
            relay_sum(2)
            open_sum(1)
            direct_sum(1)

    middle_sum(3)
    open_sum(0)
    relay_sum(1)
    relay_sum(0)
    direct_sum(0)
    middle_sum(2)
    last_sum(3)
    middle_sum(1)
    middle_sum(0)
    last_sum(2)
    last_sum(1)

    @pl.when(s != 0)
    def _():
        merge()

    last_sum(0)

    @pl.when(s == 0)
    def _():
        merge()

    pass_on()

    def hand_on(b, to):
        return remote(eval_out.at[:, cols(b, BLK)], vin.at[:, cols(b, BLK)], vs.at[b], vr.at[b], to)

    @pl.when(s == 0)
    def _():
        eval_load.wait()

    def weights(m, b):
        return merged[m, b // 2, pl.ds((b % 2) * 2, 2)].reshape(BLK, 128)

    for i in range(4):
        for a in range(2):
            gather_on(0, i, a).wait_recv()
    total = jnp.zeros((ROWS, 128), F32)
    acc = jnp.zeros((ROWS, 128), F32)
    for b in range(4):

        @pl.when(s != 0)
        def _(b=b):
            hand_on(b, partner).wait_recv()

        vt = vin[:, cols(b, BLK)]
        vf = vt.astype(F32)
        total = total + lane_fold(vf * vf)
        acc = acc + dot_nn(vt, weights(0, b))
    sv = lax.rsqrt(jnp.sum(total, axis=1, keepdims=True) * (1.0 / D) + norm_eps)
    av = gelu_value(sv * acc).astype(BF16)
    for i in range(4):
        for a in range(2):
            gather_on(1, i, a).wait_recv()
    for b in range(4):
        eval_out[:, cols(b, BLK)] = (
            vin[:, cols(b, BLK)].astype(F32) + dot_nt(av, weights(1, b))
        ).astype(BF16)

        @pl.when(c == 0)
        def _(b=b):
            hand_on(b, partner).start()

        @pl.when(s == 1)
        def _(b=b):
            hand_on(b, after).start()

    for m in range(2):
        flog_out[m] = jnp.log(dens[yl, m])
    for b in range(4):

        @pl.when(s != 3)
        def _(b=b):
            hand_on(b, partner).wait_send()

    for m in range(2):
        for j in range(1, 4):
            gather_a(m, j).wait_send()
        for i in range(4):
            for j in (1, 3):
                gather_b(m, i, j).wait_send()
            for a in range(2):
                gather_on(m, i, a).wait_send()
    for k in range(4):
        for q in range(2):

            @pl.when(jnp.logical_not(is_me(k, q)))
            def _(k=k, q=q):
                along_y(k, q).wait_send()

        give_half(k).wait_send()
        for i in range(6):
            stage_one(k, i, r2.at[k, i]).wait_send()
        for i in range(1, 4):
            stage_two(k, i).wait_send()

    @pl.when(c != yl)
    def _():
        give.wait()

    @pl.when(c == yl)
    def _():
        hold.wait()


def settle(eval_in, logp_in, flog_in, eval_out, logp_out, flog_out, ev, lo, fl, sem_in, sem_out):
    takes = [(eval_in, ev, eval_out), (logp_in, lo, logp_out), (flog_in, fl, flog_out)]
    for i, (source, held, _) in enumerate(takes):
        pltpu.make_async_copy(source, held, sem_in.at[i]).start()
    for i, (source, held, target) in enumerate(takes):
        pltpu.make_async_copy(source, held, sem_in.at[i]).wait()
        pltpu.make_async_copy(held, target, sem_out.at[i]).start()
    for i, (_, held, target) in enumerate(takes):
        pltpu.make_async_copy(held, target, sem_out.at[i]).wait()


def local(entry_states, down_proj, up_proj, label_rows, sampled_labels, eval_states):
    vmem = pl.BlockSpec(memory_space=pltpu.VMEM)
    hbm = pl.BlockSpec(memory_space=pl.ANY)
    dma = pltpu.SemaphoreType.DMA
    eval_out, logp, flog = pl.pallas_call(
        kernel,
        out_shape=(
            jax.ShapeDtypeStruct((ROWS, D), BF16),
            jax.ShapeDtypeStruct((MICRO, ROWS), F32),
            jax.ShapeDtypeStruct((2, 144, 128), F32),
        ),
        in_specs=[hbm] * 6,
        out_specs=(vmem, vmem, vmem),
        scratch_shapes=[
            pltpu.VMEM((4, 2, D, R), BF16),
            pltpu.VMEM((5, N, D), BF16),
            pltpu.VMEM((N, D), BF16),
            pltpu.VMEM((LABELS, D), BF16),
            pltpu.VMEM((MICRO, ROWS), jnp.int32),
            pltpu.VMEM((2, N, D), BF16),
            pltpu.VMEM((2, N, R), BF16),
            pltpu.VMEM((4, N, R), F32),
            pltpu.VMEM((4, N, R), BF16),
            pltpu.VMEM((4, N, 128), F32),
            pltpu.VMEM((4, 2, 2, 4, 4, 144, 128), BF16),
            pltpu.VMEM((4, 2, 4, 4, 144, 128), BF16),
            pltpu.VMEM((4, 6, 4, 144, 128), BF16),
            pltpu.VMEM((4, 2, 4, 144, 128), BF16),
            pltpu.VMEM((4, 3, 2, 144, 128), BF16),
            pltpu.VMEM((4, 2, 144, 128), BF16),
            pltpu.VMEM((4, 2, 2, 144, 128), BF16),
            pltpu.VMEM((2, 2, 144, 128), F32),
            pltpu.VMEM((4, 2, 2, 144, 128), BF16),
            pltpu.VMEM((2, 2, 4, 4, 144, 128), BF16),
            pltpu.VMEM((ROWS, D), BF16),
            pltpu.VMEM((MICRO, ROWS), F32),
            dma((32,)),
            dma((2,)), dma((2,)),
            dma((2, 2)), dma((2, 2)),
            dma((2, 4)), dma((2, 4)),
            dma((2, 4, 4)), dma((2, 4, 4)),
            dma((2, 4)), dma((2, 4)),
            dma((4,)), dma((4,)),
            dma((3,)), dma((3,)),
            dma((4,)), dma((4,)),
            dma((4, 6)), dma((4, 6)),
            dma((4, 4)), dma((4, 4)),
            dma((4, 2)), dma((4, 2)),
            dma((2, 4)), dma((2, 4)),
            dma((2, 4, 4)), dma((2, 4, 4)),
            dma((4,)), dma((4,)),
        ],
        compiler_params=pltpu.CompilerParams(
            collective_id=0, has_side_effects=True, vmem_limit_bytes=67043328
        ),
        name="merge",
    )(
        down_proj.reshape(TASKS, D, R),
        up_proj.reshape(TASKS, D, R),
        entry_states.reshape(N, D),
        sampled_labels,
        label_rows,
        eval_states,
    )
    eval_out, logp, flog = pl.pallas_call(
        settle,
        out_shape=tuple(jax.ShapeDtypeStruct(o.shape, o.dtype) for o in (eval_out, logp, flog)),
        in_specs=[hbm] * 3,
        out_specs=(hbm, hbm, hbm),
        scratch_shapes=[
            pltpu.VMEM((ROWS, D), BF16),
            pltpu.VMEM((MICRO, ROWS), F32),
            pltpu.VMEM((2, 144, 128), F32),
            dma((3,)),
            dma((3,)),
        ],
        name="settle",
    )(eval_out, logp, flog)
    return (
        eval_out[None],
        logp[None],
        flog[None],
    )


def solution(mesh):
    placed = (
        P(None, "dp", None),
        P("section", None, None, None),
        P("section", None, None, None),
        P(),
        P(None, None, "dp"),
        P("dp", None),
    )
    return jax.shard_map(
        local,
        mesh=mesh,
        in_specs=placed,
        out_specs=(
            P("section", "dp", None),
            P("section", None, "dp"),
            P("section", None, "dp", None),
        ),
        check_vma=False,
    )
```

```python
import jax
import jax.numpy as jnp
from jax import lax
from jax.experimental import pallas as pl
from jax.experimental.pallas import tpu as pltpu
from jax.sharding import PartitionSpec as P

norm_eps = 1e-06
merge_eps = 1e-06
soft_cap = 30.0
gelu_coef = 0.7978845608028654

D = 4608
R = 128
LABELS = 256
TASKS = 4
MICRO = 5
ROWS = 32
N = MICRO * ROWS
TILE = 512
BLK = D // 4
F32 = jnp.float32
BF16 = jnp.bfloat16
MESH = pl.DeviceIdType.MESH


def gelu_value(hidden):
    inner = gelu_coef * (hidden + 0.044715 * hidden * hidden * hidden)
    return 0.5 * hidden * (1.0 + jnp.tanh(inner))


def gelu_slope(hidden):
    inner = gelu_coef * (hidden + 0.044715 * hidden * hidden * hidden)
    t = jnp.tanh(inner)
    return 0.5 * (1.0 + t) + 0.5 * hidden * (1.0 - t * t) * gelu_coef * (
        1.0 + 3.0 * 0.044715 * hidden * hidden
    )


def dot_nn(a, b):
    return lax.dot_general(a, b, (((1,), (0,)), ((), ())), preferred_element_type=F32)


def dot_nt(a, b):
    return lax.dot_general(a, b, (((1,), (1,)), ((), ())), preferred_element_type=F32)


def dot_tn(a, b):
    return lax.dot_general(a, b, (((0,), (0,)), ((), ())), preferred_element_type=F32)


def over(count, body, carry):
    for i in range(count):
        carry = body(i, carry)
    return carry


def lane_fold(v):
    total = v[:, 0:128]
    for i in range(1, v.shape[1] // 128):
        total = total + v[:, i * 128 : (i + 1) * 128]
    return total


def kernel(
    down, up, entry, labels, label_rows, evals,
    eval_out, logp_out, flog_out,
    w, x, g, rows, lab, wide, narrow, hid, act, scale,
    fb, r1, r2, s2, r3, s3, r4, dens, wd, merged, vin, picked,
    load_sem, ps, pr, cs, cr, as_, ar, bs, br, bfs, bfr, os_, orr, es, er, fs, fr,
    s1s, s1r, s2s, s2r, ys, yr, gas, gar, gbs, gbr, vs, vr,
):
    s = lax.axis_index("section")
    d = lax.axis_index("dp")
    h = s // 2
    c = s % 2
    yl = d // 16
    xx = (d // 4) % 4
    zz = d % 4
    y = 2 * h + yl
    u = xx * (1 - c) + zz * c
    v = zz * (1 - c) + xx * c

    def at(h_, c_, yl_, x_, z_):
        return {"section": h_ * 2 + c_, "dp": yl_ * 16 + x_ * 4 + z_}

    def at_uv(u_, v_):
        return at(h, c, yl, u_ * (1 - c) + v_ * c, v_ * (1 - c) + u_ * c)

    def at_y(y_, core=None):
        return at(y_ // 2, c if core is None else core, y_ % 2, xx, zz)

    partner = at(h, 1 - c, yl, xx, zz)
    swap = at(h, 1 - c, 1 - yl, xx, zz)
    across = at(1 - h, c, 1 - yl, xx, zz)
    after = at(1 - h, 1 - c, yl, xx, zz)
    third = at(1 - h, 1 - c, 1 - yl, xx, zz)
    a_peers = [None] + [at_uv((u + i) % 4, v) for i in range(1, 4)]
    b_peers = [None] + [at_uv(u, (v + i) % 4) for i in range(1, 4)]
    x_peers = [None] + [at(h, c, yl, (xx + i) % 4, zz) for i in range(1, 4)]
    z_peers = [None] + [at(h, c, yl, xx, (zz + i) % 4) for i in range(1, 4)]
    y_peers = [None] + [at_y((y + i) % 4) for i in range(1, 4)]

    def remote(src, dst, send, recv, to):
        return pltpu.make_async_remote_copy(
            src_ref=src, dst_ref=dst, send_sem=send, recv_sem=recv, device_id=to, device_id_type=MESH
        )

    barrier = pltpu.get_barrier_semaphore()
    everyone = [partner, swap, after, third] + a_peers[1:] + b_peers[1:] + y_peers[1:]
    for peer in everyone:
        pl.semaphore_signal(barrier, inc=1, device_id=peer, device_id_type=MESH)
    pl.semaphore_wait(barrier, len(everyone))

    far = 3 - y
    part = D // 16
    def cross(t, m):
        place = pl.ds((((u + 2 * t) % 4) * 4 + v) * part, part)
        return remote((down, up)[m].at[far, place], w.at[s, m, place], cs.at[t, m], cr.at[t, m], across)

    for m in range(2):
        cross(0, m).start()
    beside = [
        remote(down.at[y], w.at[s, 0], ps.at[0], pr.at[0], partner),
        remote(up.at[y], w.at[s, 1], ps.at[1], pr.at[1], partner),
    ]
    moved = [
        remote(entry, x.at[0], es.at[0], er.at[0], swap),
        remote(labels, lab, es.at[1], er.at[1], swap),
    ]
    kept = [
        pltpu.make_async_copy(entry, x.at[0], load_sem.at[0]),
        pltpu.make_async_copy(labels, lab, load_sem.at[1]),
    ]

    @pl.when(c != yl)
    def _():
        for copy in moved:
            copy.start()

    @pl.when(c == yl)
    def _():
        for copy in kept:
            copy.start()

    for copy in beside:
        copy.start()
    loads = [
        pltpu.make_async_copy(down.at[y], w.at[s, 0], load_sem.at[2]),
        pltpu.make_async_copy(up.at[y], w.at[s, 1], load_sem.at[3]),
        pltpu.make_async_copy(label_rows, rows, load_sem.at[4]),
    ]
    for t in range(TASKS):
        for a in range(2):
            mine = pl.ds(pl.multiple_of((a * 16 + xx * 4 + zz) * 144, 16), 144)
            for m, whole in enumerate((down, up)):
                sem = load_sem.at[16 + 4 * t + 2 * a + m]
                loads.append(pltpu.make_async_copy(whole.at[t, mine], wd.at[t, m, a], sem))
    for copy in loads:
        copy.start()
    eval_load = pltpu.make_async_copy(evals, vin, load_sem.at[13])

    @pl.when(s == 0)
    def _():
        eval_load.start()

    lr = 2 * (1 - h) + c

    def piece(m, o, e):
        return w.at[lr, m, pl.ds((((u + o) % 4) * 4 + (v + e) % 4) * part, part)]

    def along_a(m, i):
        return remote(piece(m, 0, 0), piece(m, 0, 0), as_.at[m, i], ar.at[m, i], a_peers[i])

    def along_b(m, o, j):
        return remote(piece(m, o, 0), piece(m, o, 0), bs.at[m, o, j], br.at[m, o, j], b_peers[j])

    def further(m, o):
        view = piece(m, o, 3 if m == 0 else 1)
        return remote(view, view, bfs.at[m, o], bfr.at[m, o], b_peers[1 if m == 0 else 3])

    def to_b(o, m):
        along_b(m, o, 1).start()
        along_b(m, o, 3).start()

    def to_further(o):
        along_b(0, o, 1).wait_recv()
        further(0, o).start()
        along_b(1, o, 3).wait_recv()
        further(1, o).start()

    for m in range(2):
        cross(0, m).wait_recv()
        cross(1, m).start()
        along_a(m, 1).start()
        along_a(m, 3).start()
        to_b(0, m)
    for m in range(2):
        for o in (1, 3):
            along_a(m, 4 - o).wait_recv()
            to_b(o, m)
    to_further(0)
    for m in range(2):
        cross(1, m).wait_recv()
        to_b(2, m)
    o_sends = []
    for o in (1, 3, 2):
        to_further(o)
    for o in (0, 1, 3, 2):
        along_b(0, o, 3).wait_recv()
        along_b(1, o, 1).wait_recv()
        for m in range(2):
            further(m, o).wait_recv()
        view = w.at[lr, :, pl.ds(((u + o) % 4) * BLK, BLK)]
        copy = remote(view, view, os_.at[o], orr.at[o], partner)
        copy.start()
        o_sends.append(copy)

    @pl.when(c != yl)
    def _():
        for copy in moved:
            copy.wait()

    @pl.when(c == yl)
    def _():
        for copy in kept:
            copy.wait()

    for copy in beside:
        copy.wait()
    for copy in loads:
        copy.wait()
    for m in range(2):
        for t in range(2):
            cross(t, m).wait_send()
        for j in (1, 3):
            along_a(m, j).wait_send()
            for o in range(4):
                along_b(m, o, j).wait_send()
        for o in range(4):
            further(m, o).wait_send()
    for copy in o_sends:
        copy.wait()

    zero = jnp.zeros((N, 128), F32)

    def cols(f, size=TILE):
        return pl.ds(f * size, size)

    def first(f, carry):
        total, acc = carry
        xt = x[0, :, cols(f)]
        xf = xt.astype(F32)
        return total + lane_fold(xf * xf), acc + dot_nn(xt, w[0, 0, cols(f), :])

    total, acc = over(D // TILE, first, (zero, zero))
    for k in range(4):
        sk = lax.rsqrt(jnp.sum(total, axis=1, keepdims=True) * (1.0 / D) + norm_eps)
        hk = sk * acc
        scale[k] = jnp.broadcast_to(sk, (N, 128))
        hid[k] = hk
        ak = gelu_value(hk).astype(BF16)
        act[k] = ak

        def step(f, carry, k=k, ak=ak):
            total, acc = carry
            new = (x[k, :, cols(f)].astype(F32) + dot_nt(ak, w[k, 1, cols(f), :])).astype(BF16)
            x[k + 1, :, cols(f)] = new
            nf = new.astype(F32)
            if k < 3:
                more = dot_nn(new, w[k + 1, 0, cols(f), :])
            else:
                more = dot_nt(new, rows[:, cols(f)])
            return total + lane_fold(nf * nf), acc + more

        width = R if k < 3 else LABELS
        total, acc = over(D // TILE, step, (zero, jnp.zeros((N, width), F32)))

    sy = lax.rsqrt(jnp.sum(total, axis=1, keepdims=True) * (1.0 / D) + norm_eps)
    logits = sy * acc
    bent = jnp.tanh(logits * (1.0 / soft_cap))
    capped = soft_cap * bent
    logp = capped - jnp.log(jnp.sum(jnp.exp(capped), axis=1, keepdims=True))
    word = lax.broadcasted_iota(jnp.int32, (LABELS, ROWS), 0)
    marks = [jnp.where(word == lab[m, pl.ds(y, 1), :], 1.0, 0.0) for m in range(MICRO)]
    hot = jnp.concatenate([jnp.transpose(mark) for mark in marks], axis=0)
    for m in range(MICRO):
        part_logp = jnp.transpose(logp[m * ROWS : (m + 1) * ROWS, :])
        picked[m] = jnp.sum(part_logp * marks[m], axis=0, keepdims=True)
    give = remote(picked, logp_out, es.at[2], er.at[2], swap)
    hold = pltpu.make_async_copy(picked, logp_out, load_sem.at[14])

    @pl.when(c != yl)
    def _():
        give.start()

    @pl.when(c == yl)
    def _():
        hold.start()

    e = ((jnp.exp(logp) - hot) * (1.0 - bent * bent)).astype(BF16)
    mean = jnp.sum(e.astype(F32) * logits, axis=1, keepdims=True) * (1.0 / D)
    sm = sy * mean

    def squares(k, f, gy):
        nf = x[k, :, cols(f)].astype(F32) * scale[k][:, 0:1]
        gf = gy.astype(F32)
        wide[0, :, cols(f)] = (nf * nf).astype(BF16)
        wide[1, :, cols(f)] = (gf * gf).astype(BF16)

    def head(f, acc):
        back = dot_nn(e, rows[:, cols(f)])
        gy = (sy * (back - x[4, :, cols(f)].astype(F32) * sm)).astype(BF16)
        g[:, cols(f)] = gy
        squares(3, f, gy)
        return acc + dot_nn(gy, w[3, 1, cols(f), :])

    ga = over(D // TILE, head, zero)

    def give_half(k, m):
        return remote(fb.at[k, m], r1.at[k], fs.at[k], fr.at[k], partner)

    up_one, down_one = (u + 1) % 4, (u + 3) % 4

    def stage_one(k, i, view):
        return remote(view, r2.at[k, i], s1s.at[k, i], s1r.at[k, i], a_peers[1 if i in (0, 1, 4) else 3])

    def with_block(k, body):
        @pl.when(c == 0)
        def _():
            body(lambda t, a: fb.at[k, 0, a, t])

        @pl.when(c == 1)
        def _():
            body(lambda t, a: fb.at[k, 1, a, :, t])

    def open_sum(k):
        give_half(k, c).wait_recv()
        for a in range(2):
            for b in range(4):
                fb[k, c, a, b] = (fb[k, c, a, b].astype(F32) + r1[k, a, b].astype(F32)).astype(BF16)

        def send(view):
            stage_one(k, 4, view((u + 2) % 4, 0)).start()
            stage_one(k, 5, view((u + 2) % 4, 1)).start()

        with_block(k, send)

    def direct_sum(k):
        def send(view):
            stage_one(k, 1, view(up_one, 1)).start()
            stage_one(k, 3, view(down_one, 0)).start()

        with_block(k, send)

    def relay_sum(k):
        for i in (4, 5):
            stage_one(k, i, r2.at[k, i]).wait_recv()

        def send(view):
            for i, t, a in ((4, up_one, 0), (5, down_one, 1)):
                own_part = view(t, a)
                for b in range(4):
                    r2[k, i, b] = (r2[k, i, b].astype(F32) + own_part[b].astype(F32)).astype(BF16)
                stage_one(k, 0 if i == 4 else 2, r2.at[k, i]).start()

        with_block(k, send)

    def stage_two(k, i):
        return remote(s2.at[k, :, (v + i) % 4], r3.at[k, i - 1], s2s.at[k, i], s2r.at[k, i], b_peers[i])

    def middle_sum(k):
        for i in range(4):
            stage_one(k, i, r2.at[k, i]).wait_recv()

        def add(view):
            for a, pair in ((0, (0, 3)), (1, (1, 2))):
                own_part = view(u, a)
                for b in range(4):
                    value = own_part[b].astype(F32)
                    for i in pair:
                        value = value + r2[k, i, b].astype(F32)
                    s2[k, a, b] = value.astype(BF16)

        with_block(k, add)
        for i in (2, 1, 3):
            stage_two(k, i).start()

    def along_y(k, q):
        y_ = 2 * (k // 2) + q
        slot = (y_ + 4 - y) % 4
        return remote(s3.at[k], r4.at[slot, c], ys.at[k, q], yr.at[slot, c], at(k // 2, k % 2, q, xx, zz))

    def is_me(k, q):
        return (h == k // 2) & (c == k % 2) & (yl == q)

    def last_sum(k):
        for i in range(1, 4):
            stage_two(k, i).wait_recv()
        for a in range(2):
            value = s2[k, a, v].astype(F32)
            for i in range(3):
                value = value + r3[k, i, a].astype(F32)
            s3[k, a] = value.astype(BF16)
        for q in range(2):

            @pl.when(jnp.logical_not(is_me(k, q)))
            def _(q=q):
                along_y(k, q).start()

            @pl.when(is_me(k, q))
            def _():
                r4[0, c] = s3[k]

    def block(m, x_, z_):
        return merged.at[m, :, x_, z_]

    def gather_a(m, i):
        peers = (x_peers, z_peers)[m]
        return remote(block(m, xx, zz), block(m, xx, zz), gas.at[m, i], gar.at[m, i], peers[i])

    def gathered(m, i, e):
        x_ = (xx + 4 - i) % 4 if m == 0 else (xx + e) % 4
        z_ = (zz + 4 - i) % 4 if m == 1 else (zz + e) % 4
        return x_, z_

    def gather_b(m, i, j):
        view = block(m, *gathered(m, i, 0))
        return remote(view, view, gbs.at[m, i, j], gbr.at[m, i, j], (z_peers, x_peers)[m][j])

    def gather_on(m, i, a):
        view = merged.at[(m, a, *gathered(m, i, 3 if a == 0 else 1))]
        to = (z_peers, x_peers)[m][1 if a == 0 else 3]
        return remote(view, view, gbs.at[m, i, 2 * a], gbr.at[m, i, 2 * a], to)

    def merge():
        for i in range(4):
            for m in range(2):
                arrived = remote(r4.at[i, m], r4.at[i, m], ys.at[0, 0], yr.at[i, m], partner)
                if i:
                    arrived.wait_recv()
                else:

                    @pl.when(c != m)
                    def _(arrived=arrived):
                        arrived.wait_recv()

        for m in range(2):
            for a in range(2):
                den = jnp.zeros((144, 128), F32)
                num = jnp.zeros((144, 128), F32)
                for i in range(4):
                    t = (y + 4 - i) % 4
                    value = r4[i, m, a].astype(F32)
                    den = den + value
                    num = num + value * wd[t, m, a].astype(F32)
                den = den + merge_eps
                dens[a, m] = den
                merged[m, a, xx, zz] = (num / den).astype(BF16)
            for i in (1, 3, 2):
                gather_a(m, i).start()

    def pass_on():
        def onward(m, i):
            gather_b(m, i, 1).wait_recv()
            gather_on(m, i, 0).start()
            gather_b(m, i, 3).wait_recv()
            gather_on(m, i, 1).start()

        def direct(m, i):
            if i:
                gather_a(m, i).wait_recv()
            gather_b(m, i, 1).start()
            gather_b(m, i, 3).start()

        for i in (0, 1, 3):
            for m in range(2):
                direct(m, i)
        for m in range(2):
            onward(m, 0)
        for m in range(2):
            direct(m, 2)
        for i in (1, 3, 2):
            for m in range(2):
                onward(m, i)

    for k in (3, 2, 1, 0):
        hk = hid[k]
        sk = scale[k][:, 0:1]
        gh = (ga * gelu_slope(hk)).astype(BF16)
        ghf = gh.astype(F32)
        mean = jnp.sum(ghf * hk, axis=1, keepdims=True) * (1.0 / D)
        narrow[0] = (ghf * ghf).astype(BF16)
        af = act[k].astype(F32)
        narrow[1] = (af * af).astype(BF16)

        for m in (1 - c, c):
            thin = narrow[m]
            for b in range(4):
                value = dot_tn(wide[m, :, cols(b, BLK)], thin).astype(BF16)
                fb[k, m, b // 2, pl.ds((b % 2) * 2, 2)] = value.reshape(2, 4, 144, 128)
            if m is not c:
                give_half(k, m).start()
        if k == 0:
            break

        def step(f, acc, k=k, gh=gh, sk=sk, sm=sk * mean):
            back = dot_nt(gh, w[k, 0, cols(f), :])
            gy = (
                g[:, cols(f)].astype(F32) + (sk * back - x[k, :, cols(f)].astype(F32) * (sk * sm))
            ).astype(BF16)
            g[:, cols(f)] = gy
            squares(k - 1, f, gy)
            return acc + dot_nn(gy, w[k - 1, 1, cols(f), :])

        ga = over(D // TILE, step, zero)
        if k == 3:
            open_sum(3)
            direct_sum(3)
        if k == 2:
            relay_sum(3)
            open_sum(2)
            direct_sum(2)
        if k == 1:
            middle_sum(3)
            relay_sum(2)
            open_sum(1)
            direct_sum(1)

    open_sum(0)
    relay_sum(1)
    direct_sum(0)
    relay_sum(0)
    middle_sum(2)
    middle_sum(1)
    last_sum(3)
    last_sum(1)
    middle_sum(0)

    @pl.when(c == 1)
    def _():
        merge()

    last_sum(2)
    last_sum(0)

    @pl.when(s == 0)
    def _():
        merge()


    @pl.when(s == 2)
    def _():
        merge()

    pass_on()

    def hand_on(b, to):
        return remote(eval_out.at[:, cols(b, BLK)], vin.at[:, cols(b, BLK)], vs.at[b], vr.at[b], to)

    @pl.when(s == 0)
    def _():
        eval_load.wait()

    def weights(m, b):
        return merged[m, b // 2, pl.ds((b % 2) * 2, 2)].reshape(BLK, 128)

    for i in range(4):
        for a in range(2):
            gather_on(0, i, a).wait_recv()
    total = jnp.zeros((ROWS, 128), F32)
    acc = jnp.zeros((ROWS, 128), F32)
    for b in range(4):

        @pl.when(s != 0)
        def _(b=b):
            hand_on(b, partner).wait_recv()

        vt = vin[:, cols(b, BLK)]
        vf = vt.astype(F32)
        total = total + lane_fold(vf * vf)
        acc = acc + dot_nn(vt, weights(0, b))
    sv = lax.rsqrt(jnp.sum(total, axis=1, keepdims=True) * (1.0 / D) + norm_eps)
    av = gelu_value(sv * acc).astype(BF16)
    for i in range(4):
        for a in range(2):
            gather_on(1, i, a).wait_recv()
    for b in range(4):
        eval_out[:, cols(b, BLK)] = (
            vin[:, cols(b, BLK)].astype(F32) + dot_nt(av, weights(1, b))
        ).astype(BF16)

        @pl.when(c == 0)
        def _(b=b):
            hand_on(b, partner).start()

        @pl.when(s == 1)
        def _(b=b):
            hand_on(b, after).start()

    for m in range(2):
        flog_out[m] = jnp.log(dens[yl, m])
    for b in range(4):

        @pl.when(s != 3)
        def _(b=b):
            hand_on(b, partner).wait_send()

    for m in range(2):
        for j in range(1, 4):
            gather_a(m, j).wait_send()
        for i in range(4):
            for j in (1, 3):
                gather_b(m, i, j).wait_send()
            for a in range(2):
                gather_on(m, i, a).wait_send()
    for k in range(4):
        for q in range(2):

            @pl.when(jnp.logical_not(is_me(k, q)))
            def _(k=k, q=q):
                along_y(k, q).wait_send()

        give_half(k, 1 - c).wait_send()
        for i in range(6):
            stage_one(k, i, r2.at[k, i]).wait_send()
        for i in range(1, 4):
            stage_two(k, i).wait_send()

    @pl.when(c != yl)
    def _():
        give.wait()

    @pl.when(c == yl)
    def _():
        hold.wait()


def settle(eval_in, logp_in, flog_in, eval_out, logp_out, flog_out, ev, lo, fl, sem_in, sem_out):
    takes = [(eval_in, ev, eval_out), (logp_in, lo, logp_out), (flog_in, fl, flog_out)]
    for i, (source, held, _) in enumerate(takes):
        pltpu.make_async_copy(source, held, sem_in.at[i]).start()
    for i, (source, held, target) in enumerate(takes):
        pltpu.make_async_copy(source, held, sem_in.at[i]).wait()
        pltpu.make_async_copy(held, target, sem_out.at[i]).start()
    for i, (_, held, target) in enumerate(takes):
        pltpu.make_async_copy(held, target, sem_out.at[i]).wait()


def local(entry_states, down_proj, up_proj, label_rows, sampled_labels, eval_states):
    vmem = pl.BlockSpec(memory_space=pltpu.VMEM)
    hbm = pl.BlockSpec(memory_space=pl.ANY)
    dma = pltpu.SemaphoreType.DMA
    eval_out, logp, flog = pl.pallas_call(
        kernel,
        out_shape=(
            jax.ShapeDtypeStruct((ROWS, D), BF16),
            jax.ShapeDtypeStruct((MICRO, 1, ROWS), F32),
            jax.ShapeDtypeStruct((2, 144, 128), F32),
        ),
        in_specs=[hbm] * 6,
        out_specs=(vmem, vmem, vmem),
        scratch_shapes=[
            pltpu.VMEM((4, 2, D, R), BF16),
            pltpu.VMEM((5, N, D), BF16),
            pltpu.VMEM((N, D), BF16),
            pltpu.VMEM((LABELS, D), BF16),
            pltpu.VMEM((MICRO, TASKS, ROWS), jnp.int32),
            pltpu.VMEM((2, N, D), BF16),
            pltpu.VMEM((2, N, R), BF16),
            pltpu.VMEM((4, N, R), F32),
            pltpu.VMEM((4, N, R), BF16),
            pltpu.VMEM((4, N, 128), F32),
            pltpu.VMEM((4, 2, 2, 4, 4, 144, 128), BF16),
            pltpu.VMEM((4, 2, 4, 4, 144, 128), BF16),
            pltpu.VMEM((4, 6, 4, 144, 128), BF16),
            pltpu.VMEM((4, 2, 4, 144, 128), BF16),
            pltpu.VMEM((4, 3, 2, 144, 128), BF16),
            pltpu.VMEM((4, 2, 144, 128), BF16),
            pltpu.VMEM((4, 2, 2, 144, 128), BF16),
            pltpu.VMEM((2, 2, 144, 128), F32),
            pltpu.VMEM((4, 2, 2, 144, 128), BF16),
            pltpu.VMEM((2, 2, 4, 4, 144, 128), BF16),
            pltpu.VMEM((ROWS, D), BF16),
            pltpu.VMEM((MICRO, 1, ROWS), F32),
            dma((32,)),
            dma((2,)), dma((2,)),
            dma((2, 2)), dma((2, 2)),
            dma((2, 4)), dma((2, 4)),
            dma((2, 4, 4)), dma((2, 4, 4)),
            dma((2, 4)), dma((2, 4)),
            dma((4,)), dma((4,)),
            dma((3,)), dma((3,)),
            dma((4,)), dma((4,)),
            dma((4, 6)), dma((4, 6)),
            dma((4, 4)), dma((4, 4)),
            dma((4, 2)), dma((4, 2)),
            dma((2, 4)), dma((2, 4)),
            dma((2, 4, 4)), dma((2, 4, 4)),
            dma((4,)), dma((4,)),
        ],
        compiler_params=pltpu.CompilerParams(
            collective_id=0, has_side_effects=True, vmem_limit_bytes=67043328
        ),
        name="merge",
    )(
        down_proj.reshape(TASKS, D, R),
        up_proj.reshape(TASKS, D, R),
        entry_states.reshape(N, D),
        jnp.transpose(sampled_labels, (1, 0, 2)),
        label_rows,
        eval_states,
    )
    eval_out, logp, flog = pl.pallas_call(
        settle,
        out_shape=tuple(jax.ShapeDtypeStruct(o.shape, o.dtype) for o in (eval_out, logp, flog)),
        in_specs=[hbm] * 3,
        out_specs=(hbm, hbm, hbm),
        scratch_shapes=[
            pltpu.VMEM((ROWS, D), BF16),
            pltpu.VMEM((MICRO, 1, ROWS), F32),
            pltpu.VMEM((2, 144, 128), F32),
            dma((3,)),
            dma((3,)),
        ],
        name="settle",
    )(eval_out, logp, flog)
    return (
        eval_out[None],
        jnp.transpose(logp, (1, 0, 2)),
        flog[None],
    )


def solution(mesh):
    placed = (
        P(None, "dp", None),
        P("section", None, None, None),
        P("section", None, None, None),
        P(),
        P(None, None, "dp"),
        P("dp", None),
    )
    return jax.shard_map(
        local,
        mesh=mesh,
        in_specs=placed,
        out_specs=(
            P("section", "dp", None),
            P("section", None, "dp"),
            P("section", None, "dp", None),
        ),
        check_vma=False,
    )
```

```python
import jax
import jax.numpy as jnp
from jax import lax
from jax.experimental import pallas as pl
from jax.experimental.pallas import tpu as pltpu
from jax.sharding import PartitionSpec as P

norm_eps = 1e-06
merge_eps = 1e-06
soft_cap = 30.0
gelu_coef = 0.7978845608028654

D = 4608
R = 128
LABELS = 256
TASKS = 4
MICRO = 5
ROWS = 32
N = MICRO * ROWS
TILE = 256
BLK = D // 4
F32 = jnp.float32
BF16 = jnp.bfloat16
MESH = pl.DeviceIdType.MESH


def gelu_value(hidden):
    inner = gelu_coef * (hidden + 0.044715 * hidden * hidden * hidden)
    return 0.5 * hidden * (1.0 + jnp.tanh(inner))


def gelu_slope(hidden):
    inner = gelu_coef * (hidden + 0.044715 * hidden * hidden * hidden)
    t = jnp.tanh(inner)
    return 0.5 * (1.0 + t) + 0.5 * hidden * (1.0 - t * t) * gelu_coef * (
        1.0 + 3.0 * 0.044715 * hidden * hidden
    )


def dot_nn(a, b):
    return lax.dot_general(a, b, (((1,), (0,)), ((), ())), preferred_element_type=F32)


def dot_nt(a, b):
    return lax.dot_general(a, b, (((1,), (1,)), ((), ())), preferred_element_type=F32)


def dot_tn(a, b):
    return lax.dot_general(a, b, (((0,), (0,)), ((), ())), preferred_element_type=F32)


def over(count, body, carry):
    for i in range(count):
        carry = body(i, carry)
    return carry


def lane_fold(v):
    total = v[:, 0:128]
    for i in range(1, v.shape[1] // 128):
        total = total + v[:, i * 128 : (i + 1) * 128]
    return total


def kernel(
    down, up, entry, labels, label_rows, evals,
    eval_out, logp_out, flog_out,
    w, x, g, rows, lab, wide, narrow, hid, act, scale,
    fb, r1, r2, s2, r3, s3, r4, dens, wd, merged, vin, picked,
    load_sem, ps, pr, cs, cr, as_, ar, bs, br, bfs, bfr, os_, orr, es, er, fs, fr,
    s1s, s1r, s2s, s2r, ys, yr, gas, gar, gbs, gbr, vs, vr,
):
    s = lax.axis_index("section")
    d = lax.axis_index("dp")
    h = s // 2
    c = s % 2
    yl = d // 16
    xx = (d // 4) % 4
    zz = d % 4
    y = 2 * h + yl
    u = xx * (1 - c) + zz * c
    v = zz * (1 - c) + xx * c

    def at(h_, c_, yl_, x_, z_):
        return {"section": h_ * 2 + c_, "dp": yl_ * 16 + x_ * 4 + z_}

    def at_uv(u_, v_):
        return at(h, c, yl, u_ * (1 - c) + v_ * c, v_ * (1 - c) + u_ * c)

    def at_y(y_, core=None):
        return at(y_ // 2, c if core is None else core, y_ % 2, xx, zz)

    partner = at(h, 1 - c, yl, xx, zz)
    swap = at(h, 1 - c, 1 - yl, xx, zz)
    across = at(1 - h, c, 1 - yl, xx, zz)
    after = at(1 - h, 1 - c, yl, xx, zz)
    third = at(1 - h, 1 - c, 1 - yl, xx, zz)
    a_peers = [None] + [at_uv((u + i) % 4, v) for i in range(1, 4)]
    b_peers = [None] + [at_uv(u, (v + i) % 4) for i in range(1, 4)]
    x_peers = [None] + [at(h, c, yl, (xx + i) % 4, zz) for i in range(1, 4)]
    z_peers = [None] + [at(h, c, yl, xx, (zz + i) % 4) for i in range(1, 4)]
    y_peers = [None] + [at_y((y + i) % 4) for i in range(1, 4)]

    def remote(src, dst, send, recv, to):
        return pltpu.make_async_remote_copy(
            src_ref=src, dst_ref=dst, send_sem=send, recv_sem=recv, device_id=to, device_id_type=MESH
        )

    barrier = pltpu.get_barrier_semaphore()
    everyone = [partner, swap, after, third] + a_peers[1:] + b_peers[1:] + y_peers[1:]
    for peer in everyone:
        pl.semaphore_signal(barrier, inc=1, device_id=peer, device_id_type=MESH)
    pl.semaphore_wait(barrier, len(everyone))

    far = 3 - y
    part = D // 16
    def cross(t, m):
        place = pl.ds((((u + 2 * t) % 4) * 4 + v) * part, part)
        return remote((down, up)[m].at[far, place], w.at[s, m, place], cs.at[t, m], cr.at[t, m], across)

    for m in range(2):
        cross(0, m).start()
    beside = [
        remote(down.at[y], w.at[s, 0], ps.at[0], pr.at[0], partner),
        remote(up.at[y], w.at[s, 1], ps.at[1], pr.at[1], partner),
    ]
    moved = [
        remote(entry, x.at[0], es.at[0], er.at[0], swap),
        remote(labels, lab, es.at[1], er.at[1], swap),
    ]
    kept = [
        pltpu.make_async_copy(entry, x.at[0], load_sem.at[0]),
        pltpu.make_async_copy(labels, lab, load_sem.at[1]),
    ]

    @pl.when(c != yl)
    def _():
        for copy in moved:
            copy.start()

    @pl.when(c == yl)
    def _():
        for copy in kept:
            copy.start()

    for copy in beside:
        copy.start()
    loads = [
        pltpu.make_async_copy(down.at[y], w.at[s, 0], load_sem.at[2]),
        pltpu.make_async_copy(up.at[y], w.at[s, 1], load_sem.at[3]),
        pltpu.make_async_copy(label_rows, rows, load_sem.at[4]),
    ]
    for t in range(TASKS):
        for a in range(2):
            mine = pl.ds(pl.multiple_of((a * 16 + xx * 4 + zz) * 144, 16), 144)
            for m, whole in enumerate((down, up)):
                sem = load_sem.at[16 + 4 * t + 2 * a + m]
                loads.append(pltpu.make_async_copy(whole.at[t, mine], wd.at[t, m, a], sem))
    for copy in loads:
        copy.start()
    eval_load = pltpu.make_async_copy(evals, vin, load_sem.at[13])

    @pl.when(s == 0)
    def _():
        eval_load.start()

    lr = 2 * (1 - h) + c

    def piece(m, o, e):
        return w.at[lr, m, pl.ds((((u + o) % 4) * 4 + (v + e) % 4) * part, part)]

    def along_a(m, i):
        return remote(piece(m, 0, 0), piece(m, 0, 0), as_.at[m, i], ar.at[m, i], a_peers[i])

    def along_b(m, o, j):
        return remote(piece(m, o, 0), piece(m, o, 0), bs.at[m, o, j], br.at[m, o, j], b_peers[j])

    def further(m, o):
        view = piece(m, o, 3 if m == 0 else 1)
        return remote(view, view, bfs.at[m, o], bfr.at[m, o], b_peers[1 if m == 0 else 3])

    def to_b(o, m):
        along_b(m, o, 1).start()
        along_b(m, o, 3).start()

    def to_further(o):
        along_b(0, o, 1).wait_recv()
        further(0, o).start()
        along_b(1, o, 3).wait_recv()
        further(1, o).start()

    for m in range(2):
        cross(0, m).wait_recv()
        cross(1, m).start()
        along_a(m, 1).start()
        along_a(m, 3).start()
        to_b(0, m)
    for m in range(2):
        for o in (1, 3):
            along_a(m, 4 - o).wait_recv()
            to_b(o, m)
    to_further(0)
    for m in range(2):
        cross(1, m).wait_recv()
        to_b(2, m)
    o_sends = []
    for o in (1, 3, 2):
        to_further(o)
    for o in (0, 1, 3, 2):
        along_b(0, o, 3).wait_recv()
        along_b(1, o, 1).wait_recv()
        for m in range(2):
            further(m, o).wait_recv()
        view = w.at[lr, :, pl.ds(((u + o) % 4) * BLK, BLK)]
        copy = remote(view, view, os_.at[o], orr.at[o], partner)
        copy.start()
        o_sends.append(copy)

    @pl.when(c != yl)
    def _():
        for copy in moved:
            copy.wait()

    @pl.when(c == yl)
    def _():
        for copy in kept:
            copy.wait()

    for copy in beside:
        copy.wait()
    for copy in loads:
        copy.wait()
    for m in range(2):
        for t in range(2):
            cross(t, m).wait_send()
        for j in (1, 3):
            along_a(m, j).wait_send()
            for o in range(4):
                along_b(m, o, j).wait_send()
        for o in range(4):
            further(m, o).wait_send()
    for copy in o_sends:
        copy.wait()

    zero = jnp.zeros((N, 128), F32)

    def cols(f, size=TILE):
        return pl.ds(f * size, size)

    def first(f, carry):
        total, acc = carry
        xt = x[0, :, cols(f)]
        xf = xt.astype(F32)
        return total + lane_fold(xf * xf), acc + dot_nn(xt, w[0, 0, cols(f), :])

    total, acc = over(D // TILE, first, (zero, zero))
    for k in range(4):
        sk = lax.rsqrt(jnp.sum(total, axis=1, keepdims=True) * (1.0 / D) + norm_eps)
        hk = sk * acc
        scale[k] = jnp.broadcast_to(sk, (N, 128))
        hid[k] = hk
        ak = gelu_value(hk).astype(BF16)
        act[k] = ak

        def step(f, carry, k=k, ak=ak):
            total, acc = carry
            new = (x[k, :, cols(f)].astype(F32) + dot_nt(ak, w[k, 1, cols(f), :])).astype(BF16)
            x[k + 1, :, cols(f)] = new
            nf = new.astype(F32)
            if k < 3:
                more = dot_nn(new, w[k + 1, 0, cols(f), :])
            else:
                more = dot_nt(new, rows[:, cols(f)])
            return total + lane_fold(nf * nf), acc + more

        width = R if k < 3 else LABELS
        total, acc = over(D // TILE, step, (zero, jnp.zeros((N, width), F32)))

    sy = lax.rsqrt(jnp.sum(total, axis=1, keepdims=True) * (1.0 / D) + norm_eps)
    logits = sy * acc
    bent = jnp.tanh(logits * (1.0 / soft_cap))
    capped = soft_cap * bent
    logp = capped - jnp.log(jnp.sum(jnp.exp(capped), axis=1, keepdims=True))
    word = lax.broadcasted_iota(jnp.int32, (LABELS, ROWS), 0)
    marks = [jnp.where(word == lab[m, pl.ds(y, 1), :], 1.0, 0.0) for m in range(MICRO)]
    hot = jnp.concatenate([jnp.transpose(mark) for mark in marks], axis=0)
    for m in range(MICRO):
        part_logp = jnp.transpose(logp[m * ROWS : (m + 1) * ROWS, :])
        picked[m] = jnp.sum(part_logp * marks[m], axis=0, keepdims=True)
    give = remote(picked, logp_out, es.at[2], er.at[2], swap)
    hold = pltpu.make_async_copy(picked, logp_out, load_sem.at[14])

    @pl.when(c != yl)
    def _():
        give.start()

    @pl.when(c == yl)
    def _():
        hold.start()

    e = ((jnp.exp(logp) - hot) * (1.0 - bent * bent)).astype(BF16)
    mean = jnp.sum(e.astype(F32) * logits, axis=1, keepdims=True) * (1.0 / D)
    sm = sy * mean

    def squares(k, f, gy):
        nf = x[k, :, cols(f)].astype(F32) * scale[k][:, 0:1]
        gf = gy.astype(F32)
        wide[0, :, cols(f)] = (nf * nf).astype(BF16)
        wide[1, :, cols(f)] = (gf * gf).astype(BF16)

    def head(f, acc):
        back = dot_nn(e, rows[:, cols(f)])
        gy = (sy * (back - x[4, :, cols(f)].astype(F32) * sm)).astype(BF16)
        g[:, cols(f)] = gy
        squares(3, f, gy)
        return acc + dot_nn(gy, w[3, 1, cols(f), :])

    ga = over(D // TILE, head, zero)

    def give_half(k, m):
        return remote(fb.at[k, m], r1.at[k], fs.at[k], fr.at[k], partner)

    up_one, down_one = (u + 1) % 4, (u + 3) % 4

    def stage_one(k, i, view):
        return remote(view, r2.at[k, i], s1s.at[k, i], s1r.at[k, i], a_peers[1 if i in (0, 1, 4) else 3])

    def with_block(k, body):
        @pl.when(c == 0)
        def _():
            body(lambda t, a: fb.at[k, 0, a, t])

        @pl.when(c == 1)
        def _():
            body(lambda t, a: fb.at[k, 1, a, :, t])

    def open_sum(k):
        give_half(k, c).wait_recv()
        for a in range(2):
            for b in range(4):
                fb[k, c, a, b] = (fb[k, c, a, b].astype(F32) + r1[k, a, b].astype(F32)).astype(BF16)

        def send(view):
            stage_one(k, 4, view((u + 2) % 4, 0)).start()
            stage_one(k, 5, view((u + 2) % 4, 1)).start()

        with_block(k, send)

    def direct_sum(k):
        def send(view):
            stage_one(k, 1, view(up_one, 1)).start()
            stage_one(k, 3, view(down_one, 0)).start()

        with_block(k, send)

    def relay_sum(k):
        for i in (4, 5):
            stage_one(k, i, r2.at[k, i]).wait_recv()

        def send(view):
            for i, t, a in ((4, up_one, 0), (5, down_one, 1)):
                own_part = view(t, a)
                for b in range(4):
                    r2[k, i, b] = (r2[k, i, b].astype(F32) + own_part[b].astype(F32)).astype(BF16)
                stage_one(k, 0 if i == 4 else 2, r2.at[k, i]).start()

        with_block(k, send)

    def stage_two(k, i):
        return remote(s2.at[k, :, (v + i) % 4], r3.at[k, i - 1], s2s.at[k, i], s2r.at[k, i], b_peers[i])

    def middle_sum(k):
        for i in range(4):
            stage_one(k, i, r2.at[k, i]).wait_recv()

        def add(view):
            for a, pair in ((0, (0, 3)), (1, (1, 2))):
                own_part = view(u, a)
                for b in range(4):
                    value = own_part[b].astype(F32)
                    for i in pair:
                        value = value + r2[k, i, b].astype(F32)
                    s2[k, a, b] = value.astype(BF16)

        with_block(k, add)
        for i in (2, 1, 3):
            stage_two(k, i).start()

    def along_y(k, q):
        y_ = 2 * (k // 2) + q
        slot = (y_ + 4 - y) % 4
        return remote(s3.at[k], r4.at[slot, c], ys.at[k, q], yr.at[slot, c], at(k // 2, k % 2, q, xx, zz))

    def is_me(k, q):
        return (h == k // 2) & (c == k % 2) & (yl == q)

    def last_sum(k):
        for i in range(1, 4):
            stage_two(k, i).wait_recv()
        for a in range(2):
            value = s2[k, a, v].astype(F32)
            for i in range(3):
                value = value + r3[k, i, a].astype(F32)
            s3[k, a] = value.astype(BF16)
        for q in range(2):

            @pl.when(jnp.logical_not(is_me(k, q)))
            def _(q=q):
                along_y(k, q).start()

            @pl.when(is_me(k, q))
            def _():
                r4[0, c] = s3[k]

    def block(m, x_, z_):
        return merged.at[m, :, x_, z_]

    def gather_a(m, i):
        peers = (x_peers, z_peers)[m]
        return remote(block(m, xx, zz), block(m, xx, zz), gas.at[m, i], gar.at[m, i], peers[i])

    def gathered(m, i, e):
        x_ = (xx + 4 - i) % 4 if m == 0 else (xx + e) % 4
        z_ = (zz + 4 - i) % 4 if m == 1 else (zz + e) % 4
        return x_, z_

    def gather_b(m, i, j):
        view = block(m, *gathered(m, i, 0))
        return remote(view, view, gbs.at[m, i, j], gbr.at[m, i, j], (z_peers, x_peers)[m][j])

    def gather_on(m, i, a):
        view = merged.at[(m, a, *gathered(m, i, 3 if a == 0 else 1))]
        to = (z_peers, x_peers)[m][1 if a == 0 else 3]
        return remote(view, view, gbs.at[m, i, 2 * a], gbr.at[m, i, 2 * a], to)

    def merge():
        for i in range(4):
            for m in range(2):
                arrived = remote(r4.at[i, m], r4.at[i, m], ys.at[0, 0], yr.at[i, m], partner)
                if i:
                    arrived.wait_recv()
                else:

                    @pl.when(c != m)
                    def _(arrived=arrived):
                        arrived.wait_recv()

        for m in range(2):
            for a in range(2):
                den = jnp.zeros((144, 128), F32)
                num = jnp.zeros((144, 128), F32)
                for i in range(4):
                    t = (y + 4 - i) % 4
                    value = r4[i, m, a].astype(F32)
                    den = den + value
                    num = num + value * wd[t, m, a].astype(F32)
                den = den + merge_eps
                dens[a, m] = den
                merged[m, a, xx, zz] = (num / den).astype(BF16)
            for i in (1, 3, 2):
                gather_a(m, i).start()

    def pass_on():
        def onward(m, i):
            gather_b(m, i, 1).wait_recv()
            gather_on(m, i, 0).start()
            gather_b(m, i, 3).wait_recv()
            gather_on(m, i, 1).start()

        def direct(m, i):
            if i:
                gather_a(m, i).wait_recv()
            gather_b(m, i, 1).start()
            gather_b(m, i, 3).start()

        for i in (0, 1, 3):
            for m in range(2):
                direct(m, i)
        for m in range(2):
            onward(m, 0)
        for m in range(2):
            direct(m, 2)
        for i in (1, 3, 2):
            for m in range(2):
                onward(m, i)

    for k in (3, 2, 1, 0):
        hk = hid[k]
        sk = scale[k][:, 0:1]
        gh = (ga * gelu_slope(hk)).astype(BF16)
        ghf = gh.astype(F32)
        mean = jnp.sum(ghf * hk, axis=1, keepdims=True) * (1.0 / D)
        narrow[0] = (ghf * ghf).astype(BF16)
        af = act[k].astype(F32)
        narrow[1] = (af * af).astype(BF16)

        for m in (1 - c, c):
            thin = narrow[m]
            for b in range(4):
                value = dot_tn(wide[m, :, cols(b, BLK)], thin).astype(BF16)
                fb[k, m, b // 2, pl.ds((b % 2) * 2, 2)] = value.reshape(2, 4, 144, 128)
            if m is not c:
                give_half(k, m).start()
        if k == 0:
            break

        def step(f, acc, k=k, gh=gh, sk=sk, sm=sk * mean):
            back = dot_nt(gh, w[k, 0, cols(f), :])
            gy = (
                g[:, cols(f)].astype(F32) + (sk * back - x[k, :, cols(f)].astype(F32) * (sk * sm))
            ).astype(BF16)
            g[:, cols(f)] = gy
            squares(k - 1, f, gy)
            return acc + dot_nn(gy, w[k - 1, 1, cols(f), :])

        ga = over(D // TILE, step, zero)
        if k == 3:
            open_sum(3)
            direct_sum(3)
        if k == 2:
            relay_sum(3)
            open_sum(2)
            direct_sum(2)
        if k == 1:
            middle_sum(3)
            relay_sum(2)
            open_sum(1)
            direct_sum(1)

    open_sum(0)
    relay_sum(1)
    direct_sum(0)
    relay_sum(0)
    middle_sum(2)
    middle_sum(1)
    last_sum(3)
    last_sum(1)
    middle_sum(0)

    @pl.when(c == 1)
    def _():
        merge()

    last_sum(2)
    last_sum(0)

    @pl.when(s == 0)
    def _():
        merge()


    @pl.when(s == 2)
    def _():
        merge()

    pass_on()

    def hand_on(b, to):
        return remote(eval_out.at[:, cols(b, BLK)], vin.at[:, cols(b, BLK)], vs.at[b], vr.at[b], to)

    @pl.when(s == 0)
    def _():
        eval_load.wait()

    def weights(m, b):
        return merged[m, b // 2, pl.ds((b % 2) * 2, 2)].reshape(BLK, 128)

    for i in range(4):
        for a in range(2):
            gather_on(0, i, a).wait_recv()
    total = jnp.zeros((ROWS, 128), F32)
    acc = jnp.zeros((ROWS, 128), F32)
    for b in range(4):

        @pl.when(s != 0)
        def _(b=b):
            hand_on(b, partner).wait_recv()

        vt = vin[:, cols(b, BLK)]
        vf = vt.astype(F32)
        total = total + lane_fold(vf * vf)
        acc = acc + dot_nn(vt, weights(0, b))
    sv = lax.rsqrt(jnp.sum(total, axis=1, keepdims=True) * (1.0 / D) + norm_eps)
    av = gelu_value(sv * acc).astype(BF16)
    for i in range(4):
        for a in range(2):
            gather_on(1, i, a).wait_recv()
    for b in range(4):
        eval_out[:, cols(b, BLK)] = (
            vin[:, cols(b, BLK)].astype(F32) + dot_nt(av, weights(1, b))
        ).astype(BF16)

        @pl.when(c == 0)
        def _(b=b):
            hand_on(b, partner).start()

        @pl.when(s == 1)
        def _(b=b):
            hand_on(b, after).start()

    for m in range(2):
        flog_out[m] = jnp.log(dens[yl, m])
    for b in range(4):

        @pl.when(s != 3)
        def _(b=b):
            hand_on(b, partner).wait_send()

    for m in range(2):
        for j in range(1, 4):
            gather_a(m, j).wait_send()
        for i in range(4):
            for j in (1, 3):
                gather_b(m, i, j).wait_send()
            for a in range(2):
                gather_on(m, i, a).wait_send()
    for k in range(4):
        for q in range(2):

            @pl.when(jnp.logical_not(is_me(k, q)))
            def _(k=k, q=q):
                along_y(k, q).wait_send()

        give_half(k, 1 - c).wait_send()
        for i in range(6):
            stage_one(k, i, r2.at[k, i]).wait_send()
        for i in range(1, 4):
            stage_two(k, i).wait_send()

    @pl.when(c != yl)
    def _():
        give.wait()

    @pl.when(c == yl)
    def _():
        hold.wait()


def local(entry_states, down_proj, up_proj, label_rows, sampled_labels, eval_states):
    vmem = pl.BlockSpec(memory_space=pltpu.VMEM)
    hbm = pl.BlockSpec(memory_space=pl.ANY)
    dma = pltpu.SemaphoreType.DMA
    eval_out, logp, flog = pl.pallas_call(
        kernel,
        out_shape=(
            pltpu.VMEM((ROWS, D), BF16),
            pltpu.VMEM((MICRO, 1, ROWS), F32),
            pltpu.VMEM((2, 144, 128), F32),
        ),
        in_specs=[hbm] * 6,
        out_specs=(vmem, vmem, vmem),
        scratch_shapes=[
            pltpu.VMEM((4, 2, D, R), BF16),
            pltpu.VMEM((5, N, D), BF16),
            pltpu.VMEM((N, D), BF16),
            pltpu.VMEM((LABELS, D), BF16),
            pltpu.VMEM((MICRO, TASKS, ROWS), jnp.int32),
            pltpu.VMEM((2, N, D), BF16),
            pltpu.VMEM((2, N, R), BF16),
            pltpu.VMEM((4, N, R), F32),
            pltpu.VMEM((4, N, R), BF16),
            pltpu.VMEM((4, N, 128), F32),
            pltpu.VMEM((4, 2, 2, 4, 4, 144, 128), BF16),
            pltpu.VMEM((4, 2, 4, 4, 144, 128), BF16),
            pltpu.VMEM((4, 6, 4, 144, 128), BF16),
            pltpu.VMEM((4, 2, 4, 144, 128), BF16),
            pltpu.VMEM((4, 3, 2, 144, 128), BF16),
            pltpu.VMEM((4, 2, 144, 128), BF16),
            pltpu.VMEM((4, 2, 2, 144, 128), BF16),
            pltpu.VMEM((2, 2, 144, 128), F32),
            pltpu.VMEM((4, 2, 2, 144, 128), BF16),
            pltpu.VMEM((2, 2, 4, 4, 144, 128), BF16),
            pltpu.VMEM((ROWS, D), BF16),
            pltpu.VMEM((MICRO, 1, ROWS), F32),
            dma((32,)),
            dma((2,)), dma((2,)),
            dma((2, 2)), dma((2, 2)),
            dma((2, 4)), dma((2, 4)),
            dma((2, 4, 4)), dma((2, 4, 4)),
            dma((2, 4)), dma((2, 4)),
            dma((4,)), dma((4,)),
            dma((3,)), dma((3,)),
            dma((4,)), dma((4,)),
            dma((4, 6)), dma((4, 6)),
            dma((4, 4)), dma((4, 4)),
            dma((4, 2)), dma((4, 2)),
            dma((2, 4)), dma((2, 4)),
            dma((2, 4, 4)), dma((2, 4, 4)),
            dma((4,)), dma((4,)),
        ],
        compiler_params=pltpu.CompilerParams(
            collective_id=0, has_side_effects=True, vmem_limit_bytes=60000000
        ),
        name="merge",
    )(
        down_proj.reshape(TASKS, D, R),
        up_proj.reshape(TASKS, D, R),
        entry_states.reshape(N, D),
        jnp.transpose(sampled_labels, (1, 0, 2)),
        label_rows,
        eval_states,
    )
    return (
        eval_out[None],
        jnp.transpose(logp, (1, 0, 2)),
        flog[None],
    )


def solution(mesh):
    placed = (
        P(None, "dp", None),
        P("section", None, None, None),
        P("section", None, None, None),
        P(),
        P(None, None, "dp"),
        P("dp", None),
    )
    return jax.shard_map(
        local,
        mesh=mesh,
        in_specs=placed,
        out_specs=(
            P("section", "dp", None),
            P("section", None, "dp"),
            P("section", None, "dp", None),
        ),
        check_vma=False,
    )
```
